128 devices in a mesh: gx: 16 (over y, z_lo, core), gy: 8 (over x, z_hi).
Axes of the slice: x: 4, y: 4, z: 4 (z_hi: 2, z_lo: 2; z = z_hi * 2 + z_lo), core: 2. Of those that a mesh axis runs over, the one named last changes fastest.
Arguments:
- control: float32 [6, 4096, 2048], P(None, 'gy', 'gx'), may hold values from -6 to 6
- field_scale: float32 [6], replicated, may hold values from 0.5 to 2
- water_depth: float32 [4096, 2048], P('gy', 'gx'), may hold values from 0.5 to 4
- bed_mobility: float32 [4096, 2048], P('gy', 'gx'), may hold values from 0.1 to 1
- footprint: int32 [128, 128, 8], P(('gx', 'gy')), may hold values from 0 to 511
- instrument: int32 [128, 128, 8], P(('gx', 'gy')), may hold values from 0 to 1
- live_counts: int32 [128, 128], P(('gx', 'gy')), may hold values from 0 to 8, as said below
- observed: float32 [128, 128, 8, 128], P(('gx', 'gy')), may hold values from -6 to 6
- obs_precision: float32 [2, 128, 128], replicated, may hold values from -0.001 to 0.012, as said below
Outputs:
- gradient: float32 [6, 4096, 2048], P(None, 'gy', 'gx')
The draws below stay inside these ranges and needn't reach their ends.
Inputs may be any that keep to these rules, and one draw needn't show every extreme that they name: `live_counts`: every owner has at least one source device whose 8 slots are all live. `obs_precision`: Symmetric; every diagonal entry exceeds the sum of the magnitudes of the other entries of its row.
All inputs are finite; a program needn't handle non-finite values.
Results may differ from the reference program's by a relative error of at most 0.0001.
Values sent between devices are 32-bit elements; how exact they have to be, the bound alone decides.
No kernel may reach another device: no remote copies, remote signals or barrier semaphores. Data moves between devices by JAX's collectives and lax.ppermute only.
A program may use at most 64 MiB of HBM per device.

```python
import math
import jax
import jax.numpy as jnp
from jax import lax

F = 6
HALF = 128
BLK = 128
STEPS = 3
CAP = 8
CX = 128
CY = 512
NX = 2048
NY = 4096
OWNERS = 128
N_GY = 8


def draw_live_counts(key, part):
    key_busy = jax.random.fold_in(key, 11)
    key_heavy = jax.random.fold_in(key, 12)
    key_light = jax.random.fold_in(key, 13)
    key_full = jax.random.fold_in(key, 14)
    busy_owner = jax.random.randint(key_busy, (OWNERS, 1), 0, 4) == 0
    heavy_load = jax.random.randint(key_heavy, (OWNERS, OWNERS), CAP // 2, CAP + 1)
    light_load = jax.random.randint(key_light, (OWNERS, OWNERS), 0, CAP // 2 + 1)
    base_load = jnp.where(busy_owner, heavy_load, light_load)
    chosen = jax.random.randint(key_full, (OWNERS, 1), 0, OWNERS)
    full_slot = jnp.arange(OWNERS, dtype=jnp.int32)[None, :] == chosen
    return jnp.where(full_slot, CAP, base_load).astype(jnp.int32)


def draw_obs_precision(key, part):
    key_off = jax.random.fold_in(key, 21)
    key_diag = jax.random.fold_in(key, 22)
    random_off = jax.random.uniform(key_off, (2, BLK, BLK), jnp.float32, -1.0, 1.0)
    mirrored = 0.5 * (random_off + jnp.swapaxes(random_off, 1, 2)) / BLK
    diagonal = jax.random.uniform(key_diag, (2, BLK, 1), jnp.float32, 2.0, 3.0)
    eye_mask = jnp.arange(BLK)[:, None] == jnp.arange(BLK)[None, :]
    return (jnp.where(eye_mask[None], diagonal, mirrored) / 256.0).astype(jnp.float32)


def plant(drawn, stream_key, least, largest):
    spot = [jax.random.randint(jax.random.fold_in(stream_key, axis), (), 0, length) for axis, length in enumerate(drawn.shape)]
    main_axis = drawn.shape.index(max(drawn.shape))
    next_to = spot[:main_axis] + [(spot[main_axis] + 1) % drawn.shape[main_axis]] + spot[main_axis + 1:]
    return drawn.at[tuple(spot)].set(least).at[tuple(next_to)].set(largest)


def shard_levels(own_key, dims, shards, low, largest):
    gain, own = 1.0, jax.random.fold_in(own_key, 6)
    for axis_at, parts in shards:
        draws = jnp.exp(jax.random.uniform(jax.random.fold_in(own, axis_at), (parts,), jnp.float32, low / len(shards), largest / len(shards)))
        gain = gain * jnp.repeat(draws, dims[axis_at] // parts).reshape([-1 if axis == axis_at else 1 for axis in range(len(dims))])
    return gain


def bell_draw(stream_key, shape, scale, most, shards=(), held_as=jnp.bfloat16):
    level = shard_levels(stream_key, shape, shards, -0.22, 0.18) if shards else 1.0
    drawn = jax.random.normal(stream_key, shape, jnp.float32) * scale * level
    return jnp.minimum(jnp.maximum(drawn, -most), most).astype(held_as)


def setup_inputs(seed: int = 0) -> dict:
    splits = jax.random.split(jax.random.key(seed), 10)
    return {
        "control": bell_draw(splits[0], (F, NY, NX), 1.0, 6.0, ((1, 8), (2, 16)), jnp.float32),
        "field_scale": jnp.clip(jnp.exp(jax.random.uniform(splits[1], (F,), jnp.float32, math.log(0.5), math.log(2.0))), 0.5, 2.0),
        "water_depth": jnp.clip(jnp.exp(math.log(4.0) - 2.0794415 * jax.random.uniform(splits[2], (NY, NX), jnp.float32) ** shard_levels(splits[2], (NY, NX), ((0, 8), (1, 16)), -0.2, 0.2)), 0.5, 4.0),
        "bed_mobility": jnp.clip(jnp.exp(math.log(1.0) - 2.3025851 * jax.random.uniform(splits[3], (NY, NX), jnp.float32) ** shard_levels(splits[3], (NY, NX), ((0, 8), (1, 16)), -0.2, 0.2)), 0.1, 1.0),
        "footprint": plant(jax.random.randint(splits[4], (OWNERS, OWNERS, CAP), 0, CY * CX // BLK), jax.random.fold_in(splits[4], 1), 0, (CY * CX // BLK) - 1).astype(jnp.int32),
        "instrument": plant(jax.random.randint(splits[5], (OWNERS, OWNERS, CAP), 0, 2), jax.random.fold_in(splits[5], 1), 0, 1).astype(jnp.int32),
        "live_counts": draw_live_counts(jax.random.fold_in(splits[9], 71), 0),
        "observed": bell_draw(splits[7], (OWNERS, OWNERS, CAP, BLK), 1.0, 6.0, ((0, 128),), jnp.float32),
        "obs_precision": draw_obs_precision(jax.random.fold_in(splits[9], 71), 0),
    }


TIME_STEP = 0.2
GRAVITY = 1.0
FRICTION = 0.5
DIFFUSION = (0.4, 0.25)
SETTLING = (0.5, 0.2)

def band_table():
    window = jnp.arange(3 * HALF, dtype=jnp.int32)[:, None]
    column = jnp.arange(HALF, dtype=jnp.int32)[None, :]
    offsets = (window - column - HALF).astype(jnp.float32)
    corr_length = HALF / 2.0
    inside = jnp.abs(offsets) <= HALF
    kernel = jnp.where(inside, jnp.exp(-offsets * offsets / (2.0 * corr_length * corr_length)), 0.0)
    tap_offsets = jnp.arange(-HALF, HALF + 1, dtype=jnp.int32).astype(jnp.float32)
    norm_sum = jnp.sqrt(jnp.sum(jnp.exp(-tap_offsets * tap_offsets / (corr_length * corr_length))))
    return kernel / norm_sum

def column_pass(padded, kernel):
    channels, extent, breadth = padded.shape
    inner_count = breadth // HALF - 2
    blocks = padded.reshape(channels, extent, inner_count + 2, HALF)
    result = jnp.zeros((channels, extent, inner_count, HALF), jnp.float32)
    for offset in range(3):
        result = result + jnp.einsum('frtw,wk->frtk', blocks[:, :, offset:offset + inner_count], kernel[offset * HALF:(offset + 1) * HALF], precision=lax.Precision.HIGHEST)
    return result.reshape(channels, extent, inner_count * HALF)

def row_pass(padded, kernel):
    channels, extent, breadth = padded.shape
    inner_count = extent // HALF - 2
    blocks = padded.reshape(channels, inner_count + 2, HALF, breadth)
    result = jnp.zeros((channels, inner_count, HALF, breadth), jnp.float32)
    for offset in range(3):
        result = result + jnp.einsum('ftwc,wk->ftkc', blocks[:, offset:offset + inner_count], kernel[offset * HALF:(offset + 1) * HALF], precision=lax.Precision.HIGHEST)
    return result.reshape(channels, inner_count * HALF, breadth)

def correlate(fields, kernel):
    wide = column_pass(jnp.pad(fields, ((0, 0), (0, 0), (HALF, HALF))), kernel)
    return row_pass(jnp.pad(wide, ((0, 0), (HALF, HALF), (0, 0))), kernel)

def slope_x(padded):
    return 0.5 * (padded[:, 1:-1, 2:] - padded[:, 1:-1, :-2])

def slope_y(padded):
    return 0.5 * (padded[:, 2:, 1:-1] - padded[:, :-2, 1:-1])

def laplace(padded):
    return padded[:, 2:, 1:-1] + padded[:, :-2, 1:-1] + padded[:, 1:-1, 2:] + padded[:, 1:-1, :-2] - 4.0 * padded[:, 1:-1, 1:-1]

def pad_edges(stacked):
    return jnp.pad(stacked, ((0, 0), (1, 1), (1, 1)))

def flow_step(fields, water_depth, bed_mobility):
    height, speed_x, speed_y, bed_level, silt_one, silt_two = (fields[0], fields[1], fields[2], fields[3], fields[4], fields[5])
    fluxes = jnp.stack([water_depth * speed_x, water_depth * speed_y, bed_mobility * speed_x, bed_mobility * speed_y, silt_one, silt_two])
    padded = pad_edges(fluxes)
    along_x = slope_x(padded[:4])
    along_y = slope_y(padded[:4])
    spread = laplace(padded[4:])
    height_new = height - TIME_STEP * (along_x[0] + along_y[1])
    bed_new = bed_level - TIME_STEP * (along_x[2] + along_y[3]) + TIME_STEP * (SETTLING[0] * silt_one + SETTLING[1] * silt_two)
    silt_one_new = silt_one + TIME_STEP * DIFFUSION[0] * spread[0] - TIME_STEP * SETTLING[0] * silt_one
    silt_two_new = silt_two + TIME_STEP * DIFFUSION[1] * spread[1] - TIME_STEP * SETTLING[1] * silt_two
    surface_pad = pad_edges((height_new + bed_new)[None])
    speed_x_new = (1.0 - TIME_STEP * FRICTION) * speed_x - TIME_STEP * GRAVITY * slope_x(surface_pad)[0]
    speed_y_new = (1.0 - TIME_STEP * FRICTION) * speed_y - TIME_STEP * GRAVITY * slope_y(surface_pad)[0]
    return jnp.stack([height_new, speed_x_new, speed_y_new, bed_new, silt_one_new, silt_two_new])

def reference(control, field_scale, water_depth, bed_mobility, footprint, instrument, live_counts, observed, obs_precision):
    kernel = band_table()
    sources = jnp.arange(OWNERS, dtype=jnp.int32)
    column_base = sources // N_GY * CX
    row_base = sources % N_GY * CY
    segments = CX // BLK
    row_index = (row_base[:, None, None] + footprint // segments)[..., None]
    column_index = (column_base[:, None, None] + footprint % segments * BLK)[..., None] + jnp.arange(BLK, dtype=jnp.int32)

    def equivalents(control_in):
        fields = field_scale[:, None, None] * correlate(control_in, kernel)
        for _ in range(STEPS):
            fields = flow_step(fields, water_depth, bed_mobility)
        surface = jnp.swapaxes((fields[0] + fields[3])[row_index, column_index], 0, 1)
        bed_seen = jnp.swapaxes(fields[3][row_index, column_index], 0, 1)
        return jnp.where(instrument[..., None] == 0, surface, bed_seen)
    sensed, pullback = jax.vjp(equivalents, control)
    misfit = sensed - observed
    weighted_sar = jnp.einsum('qpcj,ij->qpci', misfit, obs_precision[0], precision=lax.Precision.HIGHEST)
    weighted_lidar = jnp.einsum('qpcj,ij->qpci', misfit, obs_precision[1], precision=lax.Precision.HIGHEST)
    live_mask = (jnp.arange(CAP, dtype=jnp.int32)[None, None, :] < live_counts[:, :, None])[..., None]
    weighted = jnp.where(live_mask, jnp.where(instrument[..., None] == 0, weighted_sar, weighted_lidar), 0.0)
    return control + pullback(weighted)[0]
```

```python
import functools
import math

import jax
import jax.numpy as jnp
import numpy as np
from jax import lax
from jax.experimental import pallas as pl
from jax.experimental.pallas import tpu as pltpu
from jax.sharding import PartitionSpec as P

HALF = 128
BLK = 128
F = 6
CX = 128
CY = 512
EXT = 8
REACH = HALF + EXT
ROWS = CY + 2 * EXT
TALL = ROWS + 16
WIDE = 256
STRIP = 640
CHUNK = 16

DT = 0.2
DECAY = 1.0 - DT * 0.5
HALF_DT = 0.5 * DT
NU = (0.4, 0.25)
WS = (0.5, 0.2)


BF = jnp.bfloat16
F32 = jnp.float32


def taps(offsets):
    length = HALF / 2.0
    steps = np.arange(-HALF, HALF + 1, dtype=np.float64)
    norm = math.sqrt(np.sum(np.exp(-steps * steps / (length * length))))
    offsets = np.asarray(offsets, np.float64)
    inside = np.abs(offsets) <= HALF
    return np.where(inside, np.exp(-offsets * offsets / (2.0 * length * length)), 0.0) / norm


def two_terms(table):
    high = table.astype(BF)
    low = (table - high.astype(np.float64)).astype(BF)
    return np.stack([high, low])


def row_table(out_rows):
    i = np.arange(out_rows)[:, None]
    j = np.arange(out_rows + 2 * HALF)[None, :]
    return two_terms(taps(j - HALF - i))


def lane_columns():
    lane = np.arange(WIDE)
    column = np.where(lane < WIDE * 3 // 4, lane, lane - WIDE)
    used = (lane < CX + EXT) | (lane >= WIDE - EXT)
    return column, used


def column_table(out_columns, used, strips=None):
    w = np.arange(CX)
    table = np.zeros((512 if strips else 384, len(out_columns)))
    out = out_columns[None, :]
    table[0:128] = taps((w - CX)[:, None] - out)
    table[128:256] = taps(w[:, None] - out)
    table[256:384] = taps((w + CX)[:, None] - out)
    if strips:
        c = np.arange(8)
        table[384:392] = taps((strips[0] + c)[:, None] - out)
        table[384 + 48 : 384 + 56] = taps((strips[1] + c)[:, None] - out)
    return two_terms(np.where(used[None, :], table, 0.0))


def terms(x):
    high = x.astype(BF)
    return high, (x - high.astype(F32)).astype(BF)


def dot(a, b):
    return jnp.dot(a, b, preferred_element_type=F32)


def lanes_of(shape):
    return lax.broadcasted_iota(jnp.int32, shape, 1)


def place(x, source, target, lane):
    moved = pltpu.roll(x, (target - source) % 128, 1) if source != target else x
    return jnp.where((lane >= target) & (lane < target + 8), moved, 0.0)


def turned(packed):
    return jnp.transpose(
        jnp.concatenate([packed, jnp.zeros((STRIP - ROWS, 128), F32)], axis=0)
    )


def stack(ref, at, flat):
    rows = flat.shape[0]
    for t in range(STRIP // 128):
        ref[at + rows * t : at + rows * (t + 1)] = flat[:, 128 * t : 128 * t + 128]


def unstack(turn, to, ref, at, rows):
    for t in range(STRIP // 128):
        turn[to : to + rows, 128 * t : 128 * t + 128] = ref[at + rows * t : at + rows * (t + 1)]


def row_forward_body(ctl, up, dn, wd, bm, table, to_left, to_right, sa, sb):
    m_high, m_low = table[0], table[1]
    lane = lanes_of((ROWS, 128))
    packed = jnp.zeros((ROWS, 128), F32)
    for pair in range(3):
        columns = []
        for f in (2 * pair, 2 * pair + 1):
            columns.append(
                jnp.concatenate(
                    [
                        up[f * REACH : (f + 1) * REACH],
                        ctl[f],
                        dn[f * REACH : (f + 1) * REACH],
                    ],
                    axis=0,
                )
            )
        high, low = terms(jnp.concatenate(columns, axis=1))
        for t in range(3):
            at = 176 * t
            xh, xl = high[at : at + 432], low[at : at + 432]
            out = dot(m_high, xh) + (dot(m_high, xl) + dot(m_low, xh))
            for k in range(2):
                to = (2 * pair + k) * ROWS + at
                half = out[:, 128 * k : 128 * k + 128]
                to_left[to : to + 176] = half
                to_right[to : to + 176] = half
    for f in range(F):
        x = to_left[f * ROWS : (f + 1) * ROWS]
        packed += place(x, 0, 8 * f, lane) + place(x, 120, 48 + 8 * f, lane)
    for k, (own, at) in enumerate(((wd, F * REACH), (bm, F * REACH + EXT))):
        x = jnp.concatenate([up[at : at + EXT], own[...], dn[at : at + EXT]], axis=0)
        packed += place(x, 0, 96 + 8 * k, lane) + place(x, 120, 112 + 8 * k, lane)
    flat = turned(packed)
    sa[...] = flat[0:48]
    sb[...] = flat[48:96]
    stack(to_left, F * ROWS, flat[96:112])
    stack(to_right, F * ROWS, flat[112:128])


def observe_body(values, index, out):
    obs = values[...]
    high, low = terms(obs)
    last = (obs - high.astype(F32) - low.astype(F32)).astype(BF)
    first_pair = jnp.concatenate([high, low], axis=1)
    second_pair = jnp.concatenate([last, jnp.ones_like(last)], axis=1)
    at = index[...]
    for block in range(8):
        row = lax.broadcasted_iota(jnp.int32, (128, 1152), 0) + 128 * block
        hot = jnp.where(row == at, 1.0, 0.0).astype(BF)
        one = dot(hot, first_pair)
        two = dot(hot, second_pair)
        out[128 * block : 128 * block + 128, :128] = one[:, :128] + (one[:, 128:] + two[:, :128])
        out[128 * block : 128 * block + 128, 128:] = two[:, 128:]


def middle_body(
    spot, scale, y, left, right, l2, r2, up, dn, wd, bm, tally, prec, table,
    to_left, to_right, ext, ext_left, ext_right,
    h, u, v, b, p1, p2, q1, q2, e, wdx, bmx, mask, turn,
):
    gx, gy, nx, ny = spot[0], spot[1], spot[2], spot[3]
    lane = lanes_of((ROWS, 128))
    turn[0:48] = l2[...]
    turn[48:96] = r2[...]
    unstack(turn, 96, left, F * ROWS, 16)
    unstack(turn, 112, right, F * ROWS, 16)
    strips = jnp.transpose(turn[...])[:ROWS]
    edge = jnp.zeros((8, WIDE), F32)
    for ref in (h, u, v, b, p1, p2, q1, q2, e, wdx, bmx, mask):
        ref[0:8] = edge
        ref[TALL - 8 : TALL] = edge
    row = lax.broadcasted_iota(jnp.int32, (ROWS, WIDE), 0) - EXT
    wide_lane = lanes_of((ROWS, WIDE))
    column = jnp.where(wide_lane < WIDE * 3 // 4, wide_lane, wide_lane - WIDE)
    row += gy * CY
    column += gx * CX
    inside = (row >= 0) & (row < ny * CY) & (column >= 0) & (column < nx * CX)
    inside_f = jnp.where(inside, 1.0, 0.0)
    mask[8 : 8 + ROWS] = inside_f
    for k, (ref, own, at) in enumerate(((wdx, wd, F * REACH), (bmx, bm, F * REACH + EXT))):
        ref[8:16, :128] = up[at : at + EXT]
        ref[16 : 16 + CY, :128] = own[...]
        ref[16 + CY : 16 + CY + EXT, :128] = dn[at : at + EXT]
        ref[8 : 8 + ROWS, 128:] = place(strips, 112 + 8 * k, 0, lane) + place(
            strips, 96 + 8 * k, 120, lane
        )
    th, tl = table[0], table[1]
    for f, ref in enumerate((h, u, v, b, p1, p2)):
        own_strip = pltpu.roll(strips, (128 - 8 * f) % 128, 1) if f else strips
        rows = slice(f * ROWS, (f + 1) * ROWS)
        x = jnp.concatenate([left[rows], y[rows], right[rows], own_strip], axis=1)
        xh, xl = terms(x)
        out = (dot(xh, th) + (dot(xl, th) + dot(xh, tl))) * scale[f]
        ref[8 : 8 + ROWS] = out * inside_f if f >= 4 else out

    def east_west(x):
        return pltpu.roll(x, WIDE - 1, 1), pltpu.roll(x, 1, 1)

    def slope_x(x):
        east, west = east_west(x)
        return east - west

    def win(ref, i):
        return ref[pl.ds(pl.multiple_of(i * CHUNK, CHUNK), CHUNK + 16)]

    def at(ref, i):
        return ref[pl.ds(pl.multiple_of(i * CHUNK + 8, 8), CHUNK)]

    def put(ref, i, value):
        ref[pl.ds(pl.multiple_of(i * CHUNK + 8, 8), CHUNK)] = value

    def centre(x):
        return x[8 : 8 + CHUNK]

    def slope_y(x):
        return x[9 : 9 + CHUNK] - x[7 : 7 + CHUNK]

    def around(x):
        east, west = east_west(centre(x))
        return (x[9 : 9 + CHUNK] + x[7 : 7 + CHUNK]) + (east + west)

    def sweep(body):
        def step(i, carry):
            body(i)
            return carry

        lax.fori_loop(0, ROWS // CHUNK, step, 0)

    def levels(s1, s2, s1_new, s2_new):
        def body(i):
            depth, mobile = win(wdx, i), win(bmx, i)
            vw = win(v, i)
            uc = at(u, i)
            w1, w2 = win(s1, i), win(s2, i)
            c1, c2 = centre(w1), centre(w2)
            hn = at(h, i) - HALF_DT * (slope_x(centre(depth) * uc) + slope_y(depth * vw))
            bn = (
                at(b, i)
                - HALF_DT * (slope_x(centre(mobile) * uc) + slope_y(mobile * vw))
                + (DT * WS[0]) * c1
                + (DT * WS[1]) * c2
            )
            put(h, i, hn)
            put(b, i, bn)
            if s1_new is not None:
                m = at(mask, i)
                put(e, i, m * (hn + bn))
                for k, (w, c, ref) in enumerate(((w1, c1, s1_new), (w2, c2, s2_new))):
                    keep = 1.0 - DT * WS[k] - 4.0 * DT * NU[k]
                    put(ref, i, m * (keep * c + (DT * NU[k]) * around(w)))

        sweep(body)

    def speeds():
        def body(i):
            ew = win(e, i)
            put(u, i, DECAY * at(u, i) - HALF_DT * slope_x(centre(ew)))
            put(v, i, DECAY * at(v, i) - HALF_DT * slope_y(ew))

        sweep(body)

    levels(p1, p2, q1, q2)
    speeds()
    levels(q1, q2, p1, p2)
    speeds()
    levels(p1, p2, None, None)

    bed = b[16 : 16 + CY, :128]
    surface = h[16 : 16 + CY, :128] + bed
    sens = []
    for k, field in enumerate((surface, bed)):
        sums = tally[k * CY : (k + 1) * CY, :128]
        count = tally[k * CY : (k + 1) * CY, 128:]
        mh, ml = terms(count * field - sums)
        rh, rl = terms(prec[k])
        sens.append(dot(mh, rh) + (dot(ml, rh) + dot(mh, rl)))
    for ref, value in ((h, sens[0]), (b, sens[0] + sens[1])):
        ref[8:16] = edge
        ref[16 + CY : 16 + CY + EXT] = edge
        ref[16 : 16 + CY, 128:] = jnp.zeros((CY, 128), F32)
        ref[16 : 16 + CY, :128] = value

    def lift():
        def body(i):
            m = at(mask, i)
            surf = (HALF_DT * m) * (slope_x(at(u, i)) + slope_y(win(v, i)))
            put(h, i, at(h, i) + surf)
            put(b, i, at(b, i) + surf)

        sweep(body)

    def back(s1, s2, s1_new, s2_new):
        def body(i):
            hw, bw = win(h, i), win(b, i)
            hc, bc = centre(hw), centre(bw)
            depth, mobile = HALF_DT * at(wdx, i), HALF_DT * at(bmx, i)
            un = depth * slope_x(hc) + mobile * slope_x(bc)
            vn = depth * slope_y(hw) + mobile * slope_y(bw)
            m = at(mask, i)
            if s1 is None:
                put(u, i, un)
                put(v, i, vn)
                put(s1_new, i, (DT * WS[0]) * bc)
                put(s2_new, i, (DT * WS[1]) * bc)
            else:
                put(u, i, DECAY * at(u, i) + un)
                put(v, i, DECAY * at(v, i) + vn)
                for k, (ref, new) in enumerate(((s1, s1_new), (s2, s2_new))):
                    w = win(ref, i)
                    keep = 1.0 - DT * WS[k] - 4.0 * DT * NU[k]
                    put(
                        new,
                        i,
                        m * (keep * centre(w) + (DT * NU[k]) * around(w) + (DT * WS[k]) * bc),
                    )

        sweep(body)

    back(None, None, p1, p2)
    lift()
    back(p1, p2, q1, q2)
    lift()
    back(q1, q2, p1, p2)

    packed = jnp.zeros((ROWS, 128), F32)
    for f, ref in enumerate((h, u, v, b, p1, p2)):
        x = ref[8 : 8 + ROWS, :128] * scale[f]
        to_left[f * ROWS : (f + 1) * ROWS] = x
        to_right[f * ROWS : (f + 1) * ROWS] = x
        x = ref[8 : 8 + ROWS, 128:] * scale[f]
        packed += place(x, 120, 8 * f, lane) + place(x, 0, 48 + 8 * f, lane)
    ext[...] = packed
    flat = turned(packed)
    ext_left[...] = flat[0:48]
    ext_right[...] = flat[48:96]
    stack(to_left, F * ROWS, flat[0:48])
    stack(to_right, F * ROWS, flat[48:96])


def column_back_body(own, ext, left, right, l2, r2, table, z, to_up, to_dn, turn):
    lane = lanes_of((ROWS, 128))
    turn[96:128] = jnp.zeros((32, STRIP), F32)
    unstack(turn, 0, left, F * ROWS, 48)
    unstack(turn, 48, right, F * ROWS, 48)
    near = jnp.transpose(turn[...])[:ROWS]
    turn[0:48] = l2[...]
    turn[48:96] = r2[...]
    far = jnp.transpose(turn[...])[:ROWS]
    mine = ext[...]
    th, tl = table[0], table[1]
    for f in range(F):
        at = slice(f * ROWS, (f + 1) * ROWS)
        west = left[at] + (place(far, 8 * f, 0, lane) + place(mine, 8 * f, 120, lane))
        here = own[at] + (place(near, 8 * f, 0, lane) + place(near, 48 + 8 * f, 120, lane))
        east = right[at] + (place(mine, 48 + 8 * f, 0, lane) + place(far, 48 + 8 * f, 120, lane))
        xh, xl = terms(jnp.concatenate([west, here, east], axis=1))
        out = dot(xh, th) + (dot(xl, th) + dot(xh, tl))
        z[f] = out
        to_up[f] = out[:REACH]
        to_dn[f] = out[ROWS - REACH :]


def row_back_body(z, up, dn, ctl, table, out):
    m_high, m_low = table[0], table[1]
    for pair in range(3):
        columns = []
        for f in (2 * pair, 2 * pair + 1):
            columns.append(
                jnp.concatenate(
                    [
                        up[f, : HALF - EXT],
                        up[f, HALF - EXT :] + z[f, : 2 * EXT],
                        z[f, 2 * EXT : ROWS - 2 * EXT],
                        z[f, ROWS - 2 * EXT :] + dn[f, : 2 * EXT],
                        dn[f, 2 * EXT :],
                    ],
                    axis=0,
                )
            )
        high, low = terms(jnp.concatenate(columns, axis=1))
        for t in range(2):
            at = 256 * t
            xh, xl = high[at : at + 512], low[at : at + 512]
            res = dot(m_high, xh) + (dot(m_high, xl) + dot(m_low, xh))
            for k in range(2):
                f = 2 * pair + k
                out[f, at : at + 256] = ctl[f, at : at + 256] + res[:, 128 * k : 128 * k + 128]


def call(body, outs, n_in, scratch=(), smem=0, name=None):
    specs = [pl.BlockSpec(memory_space=pltpu.SMEM)] * smem
    specs += [pl.BlockSpec(memory_space=pltpu.VMEM)] * (n_in - smem)
    return pl.pallas_call(
        body,
        out_shape=[jax.ShapeDtypeStruct(s, F32) for s in outs],
        in_specs=specs,
        out_specs=[pl.BlockSpec(memory_space=pltpu.VMEM)] * len(outs),
        scratch_shapes=list(scratch),
        name=name,
    )


def shift(x, axis, by):
    count = lax.axis_size(axis)
    return lax.ppermute(x, axis, [(i, i + by) for i in range(count) if 0 <= i + by < count])


def on_device(
    control, field_scale, water_depth, bed_mobility, footprint, instrument, live_counts,
    observed, obs_precision,
):
    def message(rows, edge):
        return jnp.concatenate(
            [control[:, rows].reshape(F * REACH, CX), water_depth[edge], bed_mobility[edge]]
        )

    to_dn = message(slice(CY - REACH, CY), slice(CY - EXT, CY))
    to_up = message(slice(0, REACH), slice(0, EXT))
    from_up = shift(to_dn, "gy", 1)
    from_dn = shift(to_up, "gy", -1)

    slots = instrument.shape[2]
    owners = instrument.shape[1]
    meta = jnp.zeros((owners, 1, BLK), F32)
    kinds = jnp.concatenate([instrument[0], live_counts[0][:, None]], axis=1).astype(F32)
    meta = jnp.pad(kinds[:, None, :], ((0, 0), (0, 0), (0, BLK - slots - 1)))
    parcel = jnp.concatenate([observed[0], meta], axis=1).reshape(owners * (slots + 1), BLK)
    received = lax.all_to_all(parcel, ("gx", "gy"), split_axis=0, concat_axis=0, tiled=True)
    got = received.reshape(owners, slots + 1, BLK)[:, slots, : slots + 1]
    kind = jnp.where(got[:, :slots] == 0.0, 0, CY)
    live = lax.broadcasted_iota(F32, (owners, slots), 1) < got[:, slots:]
    index = jnp.where(live, kind + footprint[0], -1).astype(jnp.int32)
    index = jnp.pad(index, ((0, 0), (0, 1)), constant_values=-1)
    index = index.reshape(1, owners * (slots + 1))
    (tally,) = call(observe_body, [(2 * CY, 256)], 2, name="observe")(received, index)

    big = F * ROWS + 16 * STRIP // 128
    y, y_right, sa, sb = call(
        row_forward_body,
        [(big, CX), (big, CX), (48, STRIP), (48, STRIP)],
        6,
        name="row_forward",
    )(control, from_up, from_dn, water_depth, bed_mobility, jnp.asarray(row_table(176)))

    left, right = shift(y_right, "gx", 1), shift(y, "gx", -1)
    l2, r2 = shift(sb, "gx", 2), shift(sa, "gx", -2)

    spot = jnp.stack(
        [
            lax.axis_index("gx"),
            lax.axis_index("gy"),
            lax.axis_size("gx"),
            lax.axis_size("gy"),
        ]
    ).astype(jnp.int32)
    columns, used = lane_columns()
    big = F * ROWS + 48 * STRIP // 128
    main, main_right, ext, ext_left, ext_right = call(
        middle_body,
        [(big, CX), (big, CX), (ROWS, CX), (48, STRIP), (48, STRIP)],
        14,
        [pltpu.VMEM((TALL, WIDE), F32)] * 12 + [pltpu.VMEM((128, STRIP), F32)],
        smem=2,
        name="middle",
    )(
        spot, field_scale, y, left, right, l2, r2, from_up, from_dn,
        water_depth, bed_mobility, tally, obs_precision,
        jnp.asarray(column_table(columns, used, (-136, 256))),
    )

    left, right = shift(main_right, "gx", 1), shift(main, "gx", -1)
    l2, r2 = shift(ext_right, "gx", 2), shift(ext_left, "gx", -2)
    z, z_up, z_dn = call(
        column_back_body,
        [(F, ROWS, CX), (F, REACH, CX), (F, REACH, CX)],
        7,
        [pltpu.VMEM((128, STRIP), F32)],
        name="column_back",
    )(
        main, ext, left, right, l2, r2,
        jnp.asarray(column_table(np.arange(CX), np.ones(CX, bool))),
    )

    from_up = shift(z_dn, "gy", 1)
    from_dn = shift(z_up, "gy", -1)
    (out,) = call(row_back_body, [(F, CY, CX)], 5, name="row_back")(
        z, from_up, from_dn, control, jnp.asarray(row_table(256))
    )
    return out


def solution(mesh):
    in_specs = (
        P(None, "gy", "gx"),
        P(),
        P("gy", "gx"),
        P("gy", "gx"),
        P(("gx", "gy"), None, None),
        P(("gx", "gy"), None, None),
        P(("gx", "gy"), None),
        P(("gx", "gy"), None, None, None),
        P(),
    )
    return jax.shard_map(
        on_device, mesh=mesh, in_specs=in_specs, out_specs=P(None, "gy", "gx"), check_vma=False
    )
```

```python
import math

import jax
import jax.numpy as jnp
import numpy as np
from jax import lax
from jax.experimental import pallas as pl
from jax.experimental.pallas import tpu as pltpu
from jax.sharding import PartitionSpec as P


HALF = 128
BLK = 128
F = 6
CX = 128
CY = 512
EXT = 8
REACH = HALF + EXT
ROWS = CY + 2 * EXT
TALL = ROWS + 16
WIDE = 256
STRIP = 640
CHUNK = ROWS

DT = 0.2
DECAY = 1.0 - DT * 0.5
HALF_DT = 0.5 * DT
NU = (0.4, 0.25)
WS = (0.5, 0.2)


BF = jnp.bfloat16
F32 = jnp.float32


def norm():
    steps = np.arange(-HALF, HALF + 1, dtype=np.float64)
    return math.sqrt(np.sum(np.exp(-steps * steps / (HALF / 2.0) ** 2)))


def taps(offset):
    far = offset.astype(F32)
    value = jnp.exp(far * far * (-0.5 / (HALF / 2.0) ** 2)) * (1.0 / norm())
    return jnp.where(jnp.abs(offset) <= HALF, value, 0.0)


def table_body(row_fwd, row_bwd, col_fwd, col_bwd):
    def axes(shape):
        return [lax.broadcasted_iota(jnp.int32, shape, d) for d in range(2)]

    def put(ref, at, value):
        high, low = terms(value)
        ref[0, at : at + value.shape[0]] = high
        ref[1, at : at + value.shape[0]] = low

    for ref in (row_fwd, row_bwd):
        i, j = axes(ref.shape[1:])
        put(ref, 0, taps(j - HALF - i))
    i, j = axes(col_bwd.shape[1:])
    put(col_bwd, 0, taps(i - CX - j))
    i, j = axes((384, WIDE))
    column = jnp.where(j < WIDE * 3 // 4, j, j - WIDE)
    used = (j < CX + EXT) | (j >= WIDE - EXT)
    put(col_fwd, 0, jnp.where(used, taps(i - CX - column), 0.0))
    i, column, used = i[:128], column[:128], used[:128]
    west, east = i < 8, (i >= 48) & (i < 56)
    offset = jnp.where(west, i - CX - EXT, i - 48 + 2 * CX) - column
    put(col_fwd, 384, jnp.where(used & (west | east), taps(offset), 0.0))


def terms(x):
    high = x.astype(BF)
    return high, (x - high.astype(F32)).astype(BF)


def dot(a, b):
    return jnp.dot(a, b, preferred_element_type=F32)


def lanes_of(shape):
    return lax.broadcasted_iota(jnp.int32, shape, 1)


def place(x, source, target, lane):
    moved = pltpu.roll(x, (target - source) % 128, 1) if source != target else x
    return jnp.where((lane >= target) & (lane < target + 8), moved, 0.0)


def turned(packed):
    return jnp.transpose(
        jnp.concatenate([packed, jnp.zeros((STRIP - ROWS, 128), F32)], axis=0)
    )


def stack(ref, at, flat):
    rows = flat.shape[0]
    for t in range(STRIP // 128):
        ref[at + rows * t : at + rows * (t + 1)] = flat[:, 128 * t : 128 * t + 128]


def unstack(turn, to, ref, at, rows):
    for t in range(STRIP // 128):
        turn[to : to + rows, 128 * t : 128 * t + 128] = ref[at + rows * t : at + rows * (t + 1)]


def row_forward_body(ctl, up, dn, wd, bm, table, to_left, to_right, sa, sb):
    m_high, m_low = table[0], table[1]
    lane = lanes_of((ROWS, 128))
    packed = jnp.zeros((ROWS, 128), F32)
    for pair in range(3):
        columns = []
        for f in (2 * pair, 2 * pair + 1):
            columns.append(
                jnp.concatenate(
                    [
                        up[f * REACH : (f + 1) * REACH],
                        ctl[f],
                        dn[f * REACH : (f + 1) * REACH],
                    ],
                    axis=0,
                )
            )
        high, low = terms(jnp.concatenate(columns, axis=1))
        for t in range(3):
            at = 176 * t
            xh, xl = high[at : at + 432], low[at : at + 432]
            out = dot(m_high, xh) + (dot(m_high, xl) + dot(m_low, xh))
            for k in range(2):
                to = (2 * pair + k) * ROWS + at
                half = out[:, 128 * k : 128 * k + 128]
                to_left[to : to + 176] = half
                to_right[to : to + 176] = half
    for f in range(F):
        x = to_left[f * ROWS : (f + 1) * ROWS]
        packed += place(x, 0, 8 * f, lane) + place(x, 120, 48 + 8 * f, lane)
    for k, (own, at) in enumerate(((wd, F * REACH), (bm, F * REACH + EXT))):
        x = jnp.concatenate([up[at : at + EXT], own[...], dn[at : at + EXT]], axis=0)
        packed += place(x, 0, 96 + 8 * k, lane) + place(x, 120, 112 + 8 * k, lane)
    flat = turned(packed)
    sa[...] = flat[0:48]
    sb[...] = flat[48:96]
    stack(to_left, F * ROWS, flat[96:112])
    stack(to_right, F * ROWS, flat[112:128])


def observe_body(values, index, out):
    obs = values[...]
    high, low = terms(obs)
    last = (obs - high.astype(F32) - low.astype(F32)).astype(BF)
    first_pair = jnp.concatenate([high, low], axis=1)
    second_pair = jnp.concatenate([last, jnp.ones_like(last)], axis=1)
    at = index[...]
    for block in range(8):
        row = lax.broadcasted_iota(jnp.int32, (128, 1152), 0) + 128 * block
        hot = jnp.where(row == at, 1.0, 0.0).astype(BF)
        one = dot(hot, first_pair)
        two = dot(hot, second_pair)
        out[128 * block : 128 * block + 128, :128] = one[:, :128] + (one[:, 128:] + two[:, :128])
        out[128 * block : 128 * block + 128, 128:] = two[:, 128:]


def middle_body(
    spot, scale, y, left, right, l2, r2, up, dn, wd, bm, tally, prec, table,
    to_left, to_right, ext, ext_left, ext_right,
    h, u, v, b, p1, p2, q1, q2, e, gw, gb, wdx, bmx, mask, turn,
):
    gx, gy, nx, ny = spot[0], spot[1], spot[2], spot[3]
    lane = lanes_of((ROWS, 128))
    turn[0:48] = l2[...]
    turn[48:96] = r2[...]
    unstack(turn, 96, left, F * ROWS, 16)
    unstack(turn, 112, right, F * ROWS, 16)
    strips = jnp.transpose(turn[...])[:ROWS]
    edge = jnp.zeros((8, WIDE), F32)
    for ref in (h, u, v, b, p1, p2, q1, q2, e, gw, gb, wdx, bmx, mask):
        ref[0:8] = edge
        ref[TALL - 8 : TALL] = edge
    row = lax.broadcasted_iota(jnp.int32, (ROWS, WIDE), 0) - EXT
    wide_lane = lanes_of((ROWS, WIDE))
    column = jnp.where(wide_lane < WIDE * 3 // 4, wide_lane, wide_lane - WIDE)
    row += gy * CY
    column += gx * CX
    inside = (row >= 0) & (row < ny * CY) & (column >= 0) & (column < nx * CX)
    inside_f = jnp.where(inside, 1.0, 0.0)
    mask[8 : 8 + ROWS] = inside_f
    for k, (ref, own, at) in enumerate(((wdx, wd, F * REACH), (bmx, bm, F * REACH + EXT))):
        ref[8:16, :128] = up[at : at + EXT]
        ref[16 : 16 + CY, :128] = own[...]
        ref[16 + CY : 16 + CY + EXT, :128] = dn[at : at + EXT]
        ref[8 : 8 + ROWS, 128:] = place(strips, 112 + 8 * k, 0, lane) + place(
            strips, 96 + 8 * k, 120, lane
        )
    th, tl = table[0], table[1]
    for f, ref in enumerate((h, u, v, b, p1, p2)):
        own_strip = pltpu.roll(strips, (128 - 8 * f) % 128, 1) if f else strips
        rows = slice(f * ROWS, (f + 1) * ROWS)
        x = jnp.concatenate([left[rows], y[rows], right[rows], own_strip], axis=1)
        xh, xl = terms(x)
        out = (dot(xh, th) + (dot(xl, th) + dot(xh, tl))) * scale[f]
        ref[8 : 8 + ROWS] = out * inside_f if f >= 4 else out
        if f == 2:
            gw[8 : 8 + ROWS] = wdx[8 : 8 + ROWS] * out
            gb[8 : 8 + ROWS] = bmx[8 : 8 + ROWS] * out

    def east_west(x):
        return pltpu.roll(x, WIDE - 1, 1), pltpu.roll(x, 1, 1)

    def slope_x(x):
        east, west = east_west(x)
        return east - west

    def at(ref, i, by=0):
        view = ref.at[pl.ds(pl.multiple_of(i * CHUNK, 8), CHUNK + 16)]
        return view[8 + by : 8 + by + CHUNK]

    def put(ref, i, value):
        ref[pl.ds(pl.multiple_of(i * CHUNK + 8, 8), CHUNK)] = value

    def slope_y(ref, i):
        return at(ref, i, 1) - at(ref, i, -1)

    def around(ref, i, centre):
        east, west = east_west(centre)
        return (at(ref, i, 1) + at(ref, i, -1)) + (east + west)

    def sweep(body):
        def step(i, carry):
            body(i)
            return carry

        lax.fori_loop(0, ROWS // CHUNK, step, 0)

    def levels(s1, s2, s1_new, s2_new):
        def body(i):
            uc = at(u, i)
            c1, c2 = at(s1, i), at(s2, i)
            hn = at(h, i) - HALF_DT * (slope_x(at(wdx, i) * uc) + slope_y(gw, i))
            bn = (
                at(b, i)
                - HALF_DT * (slope_x(at(bmx, i) * uc) + slope_y(gb, i))
                + (DT * WS[0]) * c1
                + (DT * WS[1]) * c2
            )
            put(h, i, hn)
            put(b, i, bn)
            if s1_new is not None:
                m = at(mask, i)
                put(e, i, m * (hn + bn))
                for k, (old, c, ref) in enumerate(((s1, c1, s1_new), (s2, c2, s2_new))):
                    keep = 1.0 - DT * WS[k] - 4.0 * DT * NU[k]
                    put(ref, i, m * (keep * c + (DT * NU[k]) * around(old, i, c)))

        sweep(body)

    def speeds():
        def body(i):
            put(u, i, DECAY * at(u, i) - HALF_DT * slope_x(at(e, i)))
            vn = DECAY * at(v, i) - HALF_DT * slope_y(e, i)
            put(v, i, vn)
            put(gw, i, at(wdx, i) * vn)
            put(gb, i, at(bmx, i) * vn)

        sweep(body)

    levels(p1, p2, q1, q2)
    speeds()
    levels(q1, q2, p1, p2)
    speeds()
    levels(p1, p2, None, None)

    bed = b[16 : 16 + CY, :128]
    surface = h[16 : 16 + CY, :128] + bed
    sens = []
    for k, field in enumerate((surface, bed)):
        sums = tally[k * CY : (k + 1) * CY, :128]
        count = tally[k * CY : (k + 1) * CY, 128:]
        mh, ml = terms(count * field - sums)
        rh, rl = terms(prec[k])
        sens.append(dot(mh, rh) + (dot(ml, rh) + dot(mh, rl)))
    for ref, value in ((h, sens[0]), (b, sens[0] + sens[1])):
        ref[8:16] = edge
        ref[16 + CY : 16 + CY + EXT] = edge
        ref[16 : 16 + CY, 128:] = jnp.zeros((CY, 128), F32)
        ref[16 : 16 + CY, :128] = value

    def lift():
        def body(i):
            m = at(mask, i)
            surf = (HALF_DT * m) * (slope_x(at(u, i)) + slope_y(v, i))
            put(h, i, at(h, i) + surf)
            put(b, i, at(b, i) + surf)

        sweep(body)

    def back(s1, s2, s1_new, s2_new):
        def body(i):
            hc, bc = at(h, i), at(b, i)
            depth, mobile = HALF_DT * at(wdx, i), HALF_DT * at(bmx, i)
            un = depth * slope_x(hc) + mobile * slope_x(bc)
            vn = depth * slope_y(h, i) + mobile * slope_y(b, i)
            m = at(mask, i)
            if s1 is None:
                put(u, i, un)
                put(v, i, vn)
                put(s1_new, i, (DT * WS[0]) * bc)
                put(s2_new, i, (DT * WS[1]) * bc)
            else:
                put(u, i, DECAY * at(u, i) + un)
                put(v, i, DECAY * at(v, i) + vn)
                for k, (old, new) in enumerate(((s1, s1_new), (s2, s2_new))):
                    c = at(old, i)
                    keep = 1.0 - DT * WS[k] - 4.0 * DT * NU[k]
                    put(
                        new,
                        i,
                        m * (keep * c + (DT * NU[k]) * around(old, i, c) + (DT * WS[k]) * bc),
                    )

        sweep(body)

    back(None, None, p1, p2)
    lift()
    back(p1, p2, q1, q2)
    lift()
    back(q1, q2, p1, p2)

    packed = jnp.zeros((ROWS, 128), F32)
    for f, ref in enumerate((h, u, v, b, p1, p2)):
        x = ref[8 : 8 + ROWS, :128] * scale[f]
        to_left[f * ROWS : (f + 1) * ROWS] = x
        to_right[f * ROWS : (f + 1) * ROWS] = x
        x = ref[8 : 8 + ROWS, 128:] * scale[f]
        packed += place(x, 120, 8 * f, lane) + place(x, 0, 48 + 8 * f, lane)
    ext[...] = packed
    flat = turned(packed)
    ext_left[...] = flat[0:48]
    ext_right[...] = flat[48:96]
    stack(to_left, F * ROWS, flat[0:48])
    stack(to_right, F * ROWS, flat[48:96])


def column_back_body(own, ext, left, right, l2, r2, table, z, to_up, to_dn, turn):
    lane = lanes_of((ROWS, 128))
    turn[96:128] = jnp.zeros((32, STRIP), F32)
    unstack(turn, 0, left, F * ROWS, 48)
    unstack(turn, 48, right, F * ROWS, 48)
    near = jnp.transpose(turn[...])[:ROWS]
    turn[0:48] = l2[...]
    turn[48:96] = r2[...]
    far = jnp.transpose(turn[...])[:ROWS]
    mine = ext[...]
    th, tl = table[0], table[1]
    for f in range(F):
        at = slice(f * ROWS, (f + 1) * ROWS)
        west = left[at] + (place(far, 8 * f, 0, lane) + place(mine, 8 * f, 120, lane))
        here = own[at] + (place(near, 8 * f, 0, lane) + place(near, 48 + 8 * f, 120, lane))
        east = right[at] + (place(mine, 48 + 8 * f, 0, lane) + place(far, 48 + 8 * f, 120, lane))
        xh, xl = terms(jnp.concatenate([west, here, east], axis=1))
        out = dot(xh, th) + (dot(xl, th) + dot(xh, tl))
        z[f] = out
        to_up[f] = out[:REACH]
        to_dn[f] = out[ROWS - REACH :]


def row_back_body(z, up, dn, ctl, table, out):
    m_high, m_low = table[0], table[1]
    for pair in range(3):
        columns = []
        for f in (2 * pair, 2 * pair + 1):
            columns.append(
                jnp.concatenate(
                    [
                        up[f, : HALF - EXT],
                        up[f, HALF - EXT :] + z[f, : 2 * EXT],
                        z[f, 2 * EXT : ROWS - 2 * EXT],
                        z[f, ROWS - 2 * EXT :] + dn[f, : 2 * EXT],
                        dn[f, 2 * EXT :],
                    ],
                    axis=0,
                )
            )
        high, low = terms(jnp.concatenate(columns, axis=1))
        for t in range(2):
            at = 256 * t
            xh, xl = high[at : at + 512], low[at : at + 512]
            res = dot(m_high, xh) + (dot(m_high, xl) + dot(m_low, xh))
            for k in range(2):
                f = 2 * pair + k
                out[f, at : at + 256] = ctl[f, at : at + 256] + res[:, 128 * k : 128 * k + 128]


def call(body, outs, n_in, scratch=(), smem=0, mib=16):
    specs = [pl.BlockSpec(memory_space=pltpu.SMEM)] * smem
    specs += [pl.BlockSpec(memory_space=pltpu.VMEM)] * (n_in - smem)
    return pl.pallas_call(
        body,
        out_shape=[s if hasattr(s, "dtype") else jax.ShapeDtypeStruct(s, F32) for s in outs],
        in_specs=specs,
        out_specs=[pl.BlockSpec(memory_space=pltpu.VMEM)] * len(outs),
        scratch_shapes=list(scratch),
        compiler_params=pltpu.CompilerParams(vmem_limit_bytes=mib << 20),
    )


def shift(x, axis, by):
    count = lax.axis_size(axis)
    return lax.ppermute(x, axis, [(i, i + by) for i in range(count) if 0 <= i + by < count])


def on_device(
    control, field_scale, water_depth, bed_mobility, footprint, instrument, live_counts,
    observed, obs_precision,
):
    def message(rows, edge):
        return jnp.concatenate(
            [control[:, rows].reshape(F * REACH, CX), water_depth[edge], bed_mobility[edge]]
        )

    to_dn = message(slice(CY - REACH, CY), slice(CY - EXT, CY))
    to_up = message(slice(0, REACH), slice(0, EXT))
    from_up = shift(to_dn, "gy", 1)
    from_dn = shift(to_up, "gy", -1)

    row_fwd, row_bwd, col_fwd, col_bwd = call(
        table_body,
        [
            jax.ShapeDtypeStruct((2,) + shape, BF)
            for shape in ((176, 432), (256, 512), (512, WIDE), (384, CX))
        ],
        0,
    )()

    slots = instrument.shape[2]
    owners = instrument.shape[1]
    kinds = jnp.concatenate([instrument[0], live_counts[0][:, None]], axis=1).astype(F32)
    kinds = jnp.pad(kinds[:, None, :], ((0, 0), (0, 0), (0, BLK - slots - 1)))
    parcel = jnp.concatenate([observed[0].reshape(owners, 1, slots * BLK), kinds], axis=2)
    received = lax.all_to_all(parcel, ("gx", "gy"), split_axis=0, concat_axis=0, tiled=True)
    got = received[:, 0, slots * BLK : slots * BLK + slots + 1]
    received = received.reshape(owners * (slots + 1), BLK)
    kind = jnp.where(got[:, :slots] == 0.0, 0, CY)
    live = lax.broadcasted_iota(F32, (owners, slots), 1) < got[:, slots:]
    index = jnp.where(live, kind + footprint[0], -1).astype(jnp.int32)
    index = jnp.pad(index, ((0, 0), (0, 1)), constant_values=-1)
    index = index.reshape(1, owners * (slots + 1))
    (tally,) = call(observe_body, [(2 * CY, 256)], 2)(received, index)

    big = F * ROWS + 16 * STRIP // 128
    y, y_right, sa, sb = call(
        row_forward_body, [(big, CX), (big, CX), (48, STRIP), (48, STRIP)], 6
    )(control, from_up, from_dn, water_depth, bed_mobility, row_fwd)

    left, right = shift(y_right, "gx", 1), shift(y, "gx", -1)
    l2, r2 = shift(sb, "gx", 2), shift(sa, "gx", -2)

    spot = jnp.stack(
        [
            lax.axis_index("gx"),
            lax.axis_index("gy"),
            lax.axis_size("gx"),
            lax.axis_size("gy"),
        ]
    ).astype(jnp.int32)
    big = F * ROWS + 48 * STRIP // 128
    main, main_right, ext, ext_left, ext_right = call(
        middle_body,
        [(big, CX), (big, CX), (ROWS, CX), (48, STRIP), (48, STRIP)],
        14,
        [pltpu.VMEM((TALL, WIDE), F32)] * 14 + [pltpu.VMEM((128, STRIP), F32)],
        smem=2,
        mib=40,
    )(
        spot, field_scale, y, left, right, l2, r2, from_up, from_dn,
        water_depth, bed_mobility, tally, obs_precision,
        col_fwd,
    )

    left, right = shift(main_right, "gx", 1), shift(main, "gx", -1)
    l2, r2 = shift(ext_right, "gx", 2), shift(ext_left, "gx", -2)
    z, z_up, z_dn = call(
        column_back_body,
        [(F, ROWS, CX), (F, REACH, CX), (F, REACH, CX)],
        7,
        [pltpu.VMEM((128, STRIP), F32)],
    )(
        main, ext, left, right, l2, r2,
        col_bwd,
    )

    from_up = shift(z_dn, "gy", 1)
    from_dn = shift(z_up, "gy", -1)
    (out,) = call(row_back_body, [(F, CY, CX)], 5)(z, from_up, from_dn, control, row_bwd)
    return out


def solution(mesh):
    in_specs = (
        P(None, "gy", "gx"),
        P(),
        P("gy", "gx"),
        P("gy", "gx"),
        P(("gx", "gy"), None, None),
        P(("gx", "gy"), None, None),
        P(("gx", "gy"), None),
        P(("gx", "gy"), None, None, None),
        P(),
    )
    return jax.shard_map(
        on_device, mesh=mesh, in_specs=in_specs, out_specs=P(None, "gy", "gx"), check_vma=False
    )
```

```python
import math

import jax
import jax.numpy as jnp
import numpy as np
from jax import lax
from jax.experimental import pallas as pl
from jax.experimental.pallas import tpu as pltpu
from jax.sharding import PartitionSpec as P


HALF = 128
BLK = 128
F = 6
CX = 128
CY = 512
EXT = 8
REACH = HALF + EXT
ROWS = CY + 2 * EXT
TALL = ROWS + 16
WIDE = 256
EDGE = 5
STRIP = 640
HEAD = 2
CHUNK = ROWS

DT = 0.2
DECAY = 1.0 - DT * 0.5
HALF_DT = 0.5 * DT
NU = (0.4, 0.25)
WS = (0.5, 0.2)


BF = jnp.bfloat16
F32 = jnp.float32


def norm():
    steps = np.arange(-HALF, HALF + 1, dtype=np.float64)
    return math.sqrt(np.sum(np.exp(-steps * steps / (HALF / 2.0) ** 2)))


def taps(offset):
    far = offset.astype(F32)
    value = jnp.exp(far * far * (-0.5 / (HALF / 2.0) ** 2)) * (1.0 / norm())
    return jnp.where(jnp.abs(offset) <= HALF, value, 0.0)


def table_body(row_fwd, row_bwd, col_fwd, col_bwd):
    def axes(shape):
        return [lax.broadcasted_iota(jnp.int32, shape, d) for d in range(2)]

    def put(ref, at, value):
        high, low = terms(value)
        ref[0, at : at + value.shape[0]] = high
        ref[1, at : at + value.shape[0]] = low

    for ref in (row_fwd, row_bwd):
        i, j = axes(ref.shape[1:])
        put(ref, 0, taps(j - HALF - i))
    i, j = axes(col_bwd.shape[1:])
    put(col_bwd, 0, taps(i - CX - j))
    i, j = axes((384, WIDE))
    column = jnp.where(j < WIDE * 3 // 4, j, j - WIDE)
    used = (j < CX + EDGE) | (j >= WIDE - EDGE)
    put(col_fwd, 0, jnp.where(used, taps(i - CX - column), 0.0))
    i, column, used = i[:128], column[:128], used[:128]
    west, east = i < EDGE, (i >= 32) & (i < 32 + EDGE)
    offset = jnp.where(west, i - CX - EDGE, i - 32 + 2 * CX) - column
    put(col_fwd, 384, jnp.where(used & (west | east), taps(offset), 0.0))


def terms(x):
    high = x.astype(BF)
    return high, (x - high.astype(F32)).astype(BF)


def dot(a, b):
    return jnp.dot(a, b, preferred_element_type=F32)


def lanes_of(shape):
    return lax.broadcasted_iota(jnp.int32, shape, 1)


def place(x, source, target, lane):
    moved = pltpu.roll(x, (target - source) % 128, 1) if source != target else x
    return jnp.where((lane >= target) & (lane < target + EDGE), moved, 0.0)


def turned(packed):
    return jnp.transpose(
        jnp.concatenate([packed, jnp.zeros((STRIP - ROWS, 128), F32)], axis=0)
    )


def stack(ref, at, flat):
    rows = flat.shape[0]
    for t in range(STRIP // 128):
        ref[at + rows * t : at + rows * (t + 1)] = flat[:, 128 * t : 128 * t + 128]


def unstack(turn, to, ref, at, rows):
    for t in range(STRIP // 128):
        turn[to : to + rows, 128 * t : 128 * t + 128] = ref[at + rows * t : at + rows * (t + 1)]


def row_products(pieces, table, tile, put):
    m_high, m_low = table[0], table[1]
    for pair, columns in enumerate(pieces):
        high, low = terms(jnp.concatenate(columns, axis=1))
        size = tile + 2 * HALF
        for at in range(0, high.shape[0] - size + 1, tile):
            xh, xl = high[at : at + size], low[at : at + size]
            put(pair, at, dot(m_high, xh) + (dot(m_high, xl) + dot(m_low, xh)))


def tall_pairs(ctl, first, count, up, dn):
    for f in range(0, count, 2):
        yield [
            jnp.concatenate(
                [up[k * REACH : (k + 1) * REACH], ctl[first + k], dn[k * REACH : (k + 1) * REACH]],
                axis=0,
            )
            for k in (f, f + 1)
        ]


def row_head_body(ctl, up, dn, table, y):
    def put(pair, at, out):
        for k in range(2):
            to = (2 * pair + k) * ROWS + at
            y[to : to + 176] = out[:, 128 * k : 128 * k + 128]

    row_products(tall_pairs(ctl, 0, HEAD, up, dn), table, 176, put)


def row_rest_body(ctl, up, dn, wd, bm, head, table, to_left, to_right, sa, sb):
    def put(pair, at, out):
        for k in range(2):
            to = (2 * pair + k) * ROWS + at
            half = out[:, 128 * k : 128 * k + 128]
            to_left[to : to + 176] = half
            to_right[to : to + 176] = half

    rest = F - HEAD
    row_products(tall_pairs(ctl, HEAD, rest, up, dn), table, 176, put)
    lane = lanes_of((ROWS, 128))
    packed = jnp.zeros((ROWS, 128), F32)
    for f in range(F):
        ref, at = (head, f * ROWS) if f < HEAD else (to_left, (f - HEAD) * ROWS)
        x = ref[at : at + ROWS]
        packed += place(x, 0, EDGE * f, lane) + place(x, CX - EDGE, 32 + EDGE * f, lane)
    for k, own in enumerate((wd, bm)):
        at = rest * REACH + EXT * k
        x = jnp.concatenate([up[at : at + EXT], own[...], dn[at : at + EXT]], axis=0)
        packed += place(x, 0, 64 + EDGE * k, lane) + place(x, CX - EDGE, 80 + EDGE * k, lane)
    flat = turned(packed)
    sa[...] = flat[0:32]
    sb[...] = flat[32:64]
    stack(to_left, rest * ROWS, flat[64:80])
    stack(to_right, rest * ROWS, flat[80:96])


def observe_body(values, index, out):
    obs = values[...]
    high, low = terms(obs)
    last = (obs - high.astype(F32) - low.astype(F32)).astype(BF)
    first_pair = jnp.concatenate([high, low], axis=1)
    second_pair = jnp.concatenate([last, jnp.ones_like(last)], axis=1)
    at = index[...]
    for block in range(8):
        row = lax.broadcasted_iota(jnp.int32, (128, 1152), 0) + 128 * block
        hot = jnp.where(row == at, 1.0, 0.0).astype(BF)
        one = dot(hot, first_pair)
        two = dot(hot, second_pair)
        out[128 * block : 128 * block + 128, :128] = one[:, :128] + (one[:, 128:] + two[:, :128])
        out[128 * block : 128 * block + 128, 128:] = two[:, 128:]


def middle_body(
    spot, scale, head, left_head, right_head, rest, left, right, l2, r2, up, dn, wd, bm, tally, prec, table,
    to_head, to_left, to_right, ext, ext_left, ext_right,
    h, u, v, b, p1, p2, q1, q2, e, gw, gb, wdx, bmx, mask, turn,
):
    gx, gy, nx, ny = spot[0], spot[1], spot[2], spot[3]
    lane = lanes_of((ROWS, 128))
    turn[0:32] = l2[...]
    turn[32:64] = r2[...]
    unstack(turn, 64, left, (F - HEAD) * ROWS, 16)
    unstack(turn, 80, right, (F - HEAD) * ROWS, 16)
    turn[96:128] = jnp.zeros((32, STRIP), F32)
    strips = jnp.transpose(turn[...])[:ROWS]
    edge = jnp.zeros((8, WIDE), F32)
    for ref in (h, u, v, b, p1, p2, q1, q2, e, gw, gb, wdx, bmx, mask):
        ref[0:8] = edge
        ref[TALL - 8 : TALL] = edge
    row = lax.broadcasted_iota(jnp.int32, (ROWS, WIDE), 0) - EXT
    wide_lane = lanes_of((ROWS, WIDE))
    column = jnp.where(wide_lane < WIDE * 3 // 4, wide_lane, wide_lane - WIDE)
    row += gy * CY
    column += gx * CX
    inside = (row >= 0) & (row < ny * CY) & (column >= 0) & (column < nx * CX)
    inside_f = jnp.where(inside, 1.0, 0.0)
    mask[8 : 8 + ROWS] = inside_f
    for k, (ref, own, at) in enumerate(
        ((wdx, wd, (F - HEAD) * REACH), (bmx, bm, (F - HEAD) * REACH + EXT))
    ):
        ref[8:16, :128] = up[at : at + EXT]
        ref[16 : 16 + CY, :128] = own[...]
        ref[16 + CY : 16 + CY + EXT, :128] = dn[at : at + EXT]
        ref[8 : 8 + ROWS, 128:] = place(strips, 80 + EDGE * k, 0, lane) + place(
            strips, 64 + EDGE * k, 128 - EDGE, lane
        )
    th, tl = table[0], table[1]
    for f, ref in enumerate((h, u, v, b, p1, p2)):
        own_strip = pltpu.roll(strips, 128 - EDGE * f, 1) if f else strips
        west, here, east, rows = (
            (left_head, head, right_head, f) if f < HEAD else (left, rest, right, f - HEAD)
        )
        rows = slice(rows * ROWS, (rows + 1) * ROWS)
        x = jnp.concatenate([west[rows], here[rows], east[rows], own_strip], axis=1)
        xh, xl = terms(x)
        out = (dot(xh, th) + (dot(xl, th) + dot(xh, tl))) * scale[f]
        ref[8 : 8 + ROWS] = out * inside_f if f >= 4 else out
        if f == 2:
            gw[8 : 8 + ROWS] = wdx[8 : 8 + ROWS] * out
            gb[8 : 8 + ROWS] = bmx[8 : 8 + ROWS] * out

    def east_west(x):
        return pltpu.roll(x, WIDE - 1, 1), pltpu.roll(x, 1, 1)

    def slope_x(x):
        east, west = east_west(x)
        return east - west

    def at(ref, i, by=0):
        view = ref.at[pl.ds(pl.multiple_of(i * CHUNK, 8), CHUNK + 16)]
        return view[8 + by : 8 + by + CHUNK]

    def put(ref, i, value):
        ref[pl.ds(pl.multiple_of(i * CHUNK + 8, 8), CHUNK)] = value

    def slope_y(ref, i):
        return at(ref, i, 1) - at(ref, i, -1)

    def around(ref, i, centre):
        east, west = east_west(centre)
        return (at(ref, i, 1) + at(ref, i, -1)) + (east + west)

    def sweep(body):
        def step(i, carry):
            body(i)
            return carry

        lax.fori_loop(0, ROWS // CHUNK, step, 0)

    def levels(s1, s2, s1_new, s2_new):
        def body(i):
            uc = at(u, i)
            c1, c2 = at(s1, i), at(s2, i)
            hn = at(h, i) - HALF_DT * (slope_x(at(wdx, i) * uc) + slope_y(gw, i))
            bn = (
                at(b, i)
                - HALF_DT * (slope_x(at(bmx, i) * uc) + slope_y(gb, i))
                + (DT * WS[0]) * c1
                + (DT * WS[1]) * c2
            )
            put(h, i, hn)
            put(b, i, bn)
            if s1_new is not None:
                m = at(mask, i)
                put(e, i, m * (hn + bn))
                for k, (old, c, ref) in enumerate(((s1, c1, s1_new), (s2, c2, s2_new))):
                    keep = 1.0 - DT * WS[k] - 4.0 * DT * NU[k]
                    put(ref, i, m * (keep * c + (DT * NU[k]) * around(old, i, c)))

        sweep(body)

    def speeds():
        def body(i):
            put(u, i, DECAY * at(u, i) - HALF_DT * slope_x(at(e, i)))
            vn = DECAY * at(v, i) - HALF_DT * slope_y(e, i)
            put(v, i, vn)
            put(gw, i, at(wdx, i) * vn)
            put(gb, i, at(bmx, i) * vn)

        sweep(body)

    levels(p1, p2, q1, q2)
    speeds()
    levels(q1, q2, p1, p2)
    speeds()
    levels(p1, p2, None, None)

    bed = b[16 : 16 + CY, :128]
    surface = h[16 : 16 + CY, :128] + bed
    sens = []
    for k, field in enumerate((surface, bed)):
        sums = tally[k * CY : (k + 1) * CY, :128]
        count = tally[k * CY : (k + 1) * CY, 128:]
        mh, ml = terms(count * field - sums)
        rh, rl = terms(prec[k])
        sens.append(dot(mh, rh) + (dot(ml, rh) + dot(mh, rl)))
    for ref, value in ((h, sens[0]), (b, sens[0] + sens[1])):
        ref[8:16] = edge
        ref[16 + CY : 16 + CY + EXT] = edge
        ref[16 : 16 + CY, 128:] = jnp.zeros((CY, 128), F32)
        ref[16 : 16 + CY, :128] = value

    def lift():
        def body(i):
            m = at(mask, i)
            surf = (HALF_DT * m) * (slope_x(at(u, i)) + slope_y(v, i))
            put(h, i, at(h, i) + surf)
            put(b, i, at(b, i) + surf)

        sweep(body)

    def back(s1, s2, s1_new, s2_new):
        def body(i):
            hc, bc = at(h, i), at(b, i)
            depth, mobile = HALF_DT * at(wdx, i), HALF_DT * at(bmx, i)
            un = depth * slope_x(hc) + mobile * slope_x(bc)
            vn = depth * slope_y(h, i) + mobile * slope_y(b, i)
            m = at(mask, i)
            if s1 is None:
                put(u, i, un)
                put(v, i, vn)
                put(s1_new, i, (DT * WS[0]) * bc)
                put(s2_new, i, (DT * WS[1]) * bc)
            else:
                put(u, i, DECAY * at(u, i) + un)
                put(v, i, DECAY * at(v, i) + vn)
                for k, (old, new) in enumerate(((s1, s1_new), (s2, s2_new))):
                    c = at(old, i)
                    keep = 1.0 - DT * WS[k] - 4.0 * DT * NU[k]
                    put(
                        new,
                        i,
                        m * (keep * c + (DT * NU[k]) * around(old, i, c) + (DT * WS[k]) * bc),
                    )

        sweep(body)

    back(None, None, p1, p2)
    lift()
    back(p1, p2, q1, q2)
    lift()
    back(q1, q2, p1, p2)

    packed = jnp.zeros((ROWS, 128), F32)
    for f, ref in enumerate((h, u, v, b, p1, p2)):
        x = ref[8 : 8 + ROWS, :128] * scale[f]
        if f < HEAD:
            to_head[f * ROWS : (f + 1) * ROWS] = x
        else:
            to_left[(f - HEAD) * ROWS : (f - HEAD + 1) * ROWS] = x
            to_right[(f - HEAD) * ROWS : (f - HEAD + 1) * ROWS] = x
        x = ref[8 : 8 + ROWS, 128:] * scale[f]
        packed += place(x, 128 - EDGE, EDGE * f, lane) + place(x, 0, 32 + EDGE * f, lane)
    ext[...] = packed
    flat = turned(packed)
    ext_left[...] = flat[0:32]
    ext_right[...] = flat[32:64]
    stack(to_left, (F - HEAD) * ROWS, flat[0:32])
    stack(to_right, (F - HEAD) * ROWS, flat[32:64])


def column_back(fields, first, own, left, right, mine, near, far, table, z, to_up, to_dn):
    lane = lanes_of((ROWS, 128))
    th, tl = table[0], table[1]
    for k in range(fields):
        at = slice(k * ROWS, (k + 1) * ROWS)
        one, two = EDGE * (first + k), 32 + EDGE * (first + k)
        west = left[at] + (place(far, one, 0, lane) + place(mine, one, CX - EDGE, lane))
        here = own[at] + (place(near, one, 0, lane) + place(near, two, CX - EDGE, lane))
        east = right[at] + (place(mine, two, 0, lane) + place(far, two, CX - EDGE, lane))
        xh, xl = terms(jnp.concatenate([west, here, east], axis=1))
        out = dot(xh, th) + (dot(xl, th) + dot(xh, tl))
        z[k] = out
        to_up[k] = out[:REACH]
        to_dn[k] = out[ROWS - REACH :]


def column_rest_body(
    own, ext, left, right, l2, r2, table, z, to_up, to_dn, near_out, far_out, turn
):
    turn[64:128] = jnp.zeros((64, STRIP), F32)
    unstack(turn, 0, left, (F - HEAD) * ROWS, 32)
    unstack(turn, 32, right, (F - HEAD) * ROWS, 32)
    near = jnp.transpose(turn[...])[:ROWS]
    turn[0:32] = l2[...]
    turn[32:64] = r2[...]
    far = jnp.transpose(turn[...])[:ROWS]
    near_out[...] = near
    far_out[...] = far
    column_back(F - HEAD, HEAD, own, left, right, ext[...], near, far, table, z, to_up, to_dn)


def column_head_body(own, ext, left, right, near, far, table, z, to_up, to_dn):
    column_back(HEAD, 0, own, left, right, ext[...], near[...], far[...], table, z, to_up, to_dn)


def row_back_body(z_head, up_head, dn_head, z_rest, up_rest, dn_rest, ctl, table, out):
    def pairs():
        for f in range(0, F, 2):
            columns = []
            for k in (f, f + 1):
                z, up, dn, at = (
                    (z_head, up_head, dn_head, k)
                    if k < HEAD
                    else (z_rest, up_rest, dn_rest, k - HEAD)
                )
                columns.append(
                    jnp.concatenate(
                        [
                            up[at, : HALF - EXT],
                            up[at, HALF - EXT :] + z[at, : 2 * EXT],
                            z[at, 2 * EXT : ROWS - 2 * EXT],
                            z[at, ROWS - 2 * EXT :] + dn[at, : 2 * EXT],
                            dn[at, 2 * EXT :],
                        ],
                        axis=0,
                    )
                )
            yield columns

    def put(pair, at, res):
        for k in range(2):
            f = 2 * pair + k
            out[f, at : at + 256] = ctl[f, at : at + 256] + res[:, 128 * k : 128 * k + 128]

    row_products(pairs(), table, 256, put)


def call(body, outs, n_in, scratch=(), smem=0, mib=16):
    specs = [pl.BlockSpec(memory_space=pltpu.SMEM)] * smem
    specs += [pl.BlockSpec(memory_space=pltpu.VMEM)] * (n_in - smem)
    return pl.pallas_call(
        body,
        out_shape=[s if hasattr(s, "dtype") else jax.ShapeDtypeStruct(s, F32) for s in outs],
        in_specs=specs,
        out_specs=[pl.BlockSpec(memory_space=pltpu.VMEM)] * len(outs),
        scratch_shapes=list(scratch),
        compiler_params=pltpu.CompilerParams(vmem_limit_bytes=mib << 20),
    )


def shift(x, axis, by):
    count = lax.axis_size(axis)
    return lax.ppermute(x, axis, [(i, i + by) for i in range(count) if 0 <= i + by < count])


def on_device(
    control, field_scale, water_depth, bed_mobility, footprint, instrument, live_counts,
    observed, obs_precision,
):
    def head_rows(rows):
        return control[:HEAD, rows].reshape(HEAD * REACH, CX)

    def rest_rows(rows, edge):
        return jnp.concatenate(
            [
                control[HEAD:, rows].reshape((F - HEAD) * REACH, CX),
                water_depth[edge],
                bed_mobility[edge],
            ]
        )

    last, first = slice(CY - REACH, CY), slice(0, REACH)
    up_head = shift(head_rows(last), "gy", 1)
    dn_head = shift(head_rows(first), "gy", -1)
    up_rest = shift(rest_rows(last, slice(CY - EXT, CY)), "gy", 1)
    dn_rest = shift(rest_rows(first, slice(0, EXT)), "gy", -1)

    row_fwd, row_bwd, col_fwd, col_bwd = call(
        table_body,
        [
            jax.ShapeDtypeStruct((2,) + shape, BF)
            for shape in ((176, 432), (256, 512), (512, WIDE), (384, CX))
        ],
        0,
    )()

    slots = instrument.shape[2]
    owners = instrument.shape[1]
    kinds = jnp.concatenate([instrument[0], live_counts[0][:, None]], axis=1).astype(F32)
    kinds = jnp.pad(kinds[:, None, :], ((0, 0), (0, 0), (0, BLK - slots - 1)))
    parcel = jnp.concatenate([observed[0].reshape(owners, 1, slots * BLK), kinds], axis=2)
    received = lax.all_to_all(parcel, ("gx", "gy"), split_axis=0, concat_axis=0, tiled=True)
    got = received[:, 0, slots * BLK : slots * BLK + slots + 1]
    received = received.reshape(owners * (slots + 1), BLK)
    kind = jnp.where(got[:, :slots] == 0.0, 0, CY)
    live = lax.broadcasted_iota(F32, (owners, slots), 1) < got[:, slots:]
    index = jnp.where(live, kind + footprint[0], -1).astype(jnp.int32)
    index = jnp.pad(index, ((0, 0), (0, 1)), constant_values=-1)
    index = index.reshape(1, owners * (slots + 1))
    (tally,) = call(observe_body, [(2 * CY, 256)], 2)(received, index)

    rest = F - HEAD
    (head,) = call(row_head_body, [(HEAD * ROWS, CX)], 4)(control, up_head, dn_head, row_fwd)
    left_head = shift(head, "gx", 1)
    right_head = shift(head, "gx", -1)
    big = rest * ROWS + 16 * STRIP // 128
    y, y_right, sa, sb = call(
        row_rest_body, [(big, CX), (big, CX), (32, STRIP), (32, STRIP)], 7
    )(control, up_rest, dn_rest, water_depth, bed_mobility, head, row_fwd)
    l2 = shift(sb, "gx", 2)
    r2 = shift(sa, "gx", -2)
    left = shift(y_right, "gx", 1)
    right = shift(y, "gx", -1)

    spot = jnp.stack(
        [
            lax.axis_index("gx"),
            lax.axis_index("gy"),
            lax.axis_size("gx"),
            lax.axis_size("gy"),
        ]
    ).astype(jnp.int32)
    big = rest * ROWS + 32 * STRIP // 128
    main_head, main, main_right, ext, ext_left, ext_right = call(
        middle_body,
        [
            (HEAD * ROWS, CX), (big, CX), (big, CX), (ROWS, CX), (32, STRIP), (32, STRIP),
        ],
        17,
        [pltpu.VMEM((TALL, WIDE), F32)] * 14 + [pltpu.VMEM((128, STRIP), F32)],
        smem=2,
        mib=40,
    )(
        spot, field_scale, head, left_head, right_head, y, left, right, l2, r2,
        up_rest, dn_rest, water_depth, bed_mobility, tally, obs_precision, col_fwd,
    )

    l2 = shift(ext_right, "gx", 2)
    r2 = shift(ext_left, "gx", -2)
    left = shift(main_right, "gx", 1)
    right = shift(main, "gx", -1)
    left_head = shift(main_head, "gx", 1)
    right_head = shift(main_head, "gx", -1)
    z_rest, to_up, to_dn, near, far = call(
        column_rest_body,
        [(rest, ROWS, CX), (rest, REACH, CX), (rest, REACH, CX), (ROWS, CX), (ROWS, CX)],
        7,
        [pltpu.VMEM((128, STRIP), F32)],
    )(main, ext, left, right, l2, r2, col_bwd)
    up_rest, dn_rest = shift(to_dn, "gy", 1), shift(to_up, "gy", -1)
    z_head, to_up, to_dn = call(
        column_head_body, [(HEAD, ROWS, CX), (HEAD, REACH, CX), (HEAD, REACH, CX)], 7
    )(main_head, ext, left_head, right_head, near, far, col_bwd)
    up_head, dn_head = shift(to_dn, "gy", 1), shift(to_up, "gy", -1)
    (out,) = call(row_back_body, [(F, CY, CX)], 8)(
        z_head, up_head, dn_head, z_rest, up_rest, dn_rest, control, row_bwd
    )
    return out


def solution(mesh):
    in_specs = (
        P(None, "gy", "gx"),
        P(),
        P("gy", "gx"),
        P("gy", "gx"),
        P(("gx", "gy"), None, None),
        P(("gx", "gy"), None, None),
        P(("gx", "gy"), None),
        P(("gx", "gy"), None, None, None),
        P(),
    )
    return jax.shard_map(
        on_device, mesh=mesh, in_specs=in_specs, out_specs=P(None, "gy", "gx"), check_vma=False
    )
```

```python
import math

import jax
import jax.numpy as jnp
import numpy as np
from jax import lax
from jax.experimental import pallas as pl
from jax.experimental.pallas import tpu as pltpu
from jax.sharding import PartitionSpec as P


HALF = 128
BLK = 128
F = 6
CX = 128
CY = 512
EXT = 8
REACH = HALF + EXT
ROWS = CY + 2 * EXT
TALL = ROWS + 16
WIDE = 256
EDGE = 5
STRIP = 640
HEAD = 2
CHUNK = ROWS

DT = 0.2
DECAY = 1.0 - DT * 0.5
HALF_DT = 0.5 * DT
NU = (0.4, 0.25)
WS = (0.5, 0.2)


GX, GY = "gx", "gy"
MID = 26
BF = jnp.bfloat16
F32 = jnp.float32


def norm():
    steps = np.arange(-HALF, HALF + 1, dtype=np.float64)
    return math.sqrt(np.sum(np.exp(-steps * steps / (HALF / 2.0) ** 2)))


def taps(offset):
    far = offset.astype(F32)
    value = jnp.exp(far * far * (-0.5 / (HALF / 2.0) ** 2)) * (1.0 / norm())
    return jnp.where(jnp.abs(offset) <= HALF, value, 0.0)


def axes(shape):
    return [lax.broadcasted_iota(jnp.int32, shape, d) for d in range(2)]


def put_terms(ref, value):
    high, low = terms(value)
    ref[0] = high
    ref[1] = low


def row_table_body(ref):
    i, j = axes(ref.shape[1:])
    put_terms(ref, taps(j - HALF - i))


def table_body(row_bwd, col_fwd, col_ext, col_bwd):
    row_table_body(row_bwd)
    i, j = axes(col_bwd.shape[1:])
    put_terms(col_bwd, taps(i - CX - j))
    i, j = axes((3 * CX, WIDE))
    column = jnp.where(j < WIDE * 3 // 4, j, j - WIDE)
    used = (j < CX + EDGE) | (j >= WIDE - EDGE)
    source = jnp.where(i < CX, i - CX, jnp.where(i < 2 * CX, i, i - 2 * CX))
    put_terms(col_fwd, jnp.where(used, taps(source - column), 0.0))
    i, j = axes((CX, CX))
    total = jnp.zeros((CX, CX), F32)
    for f in range(F):
        for strip, lane, gap in ((EDGE * f, 8 * f, -CX), (32 + EDGE * f, 64 + 8 * f, CX)):
            hit = (i >= strip) & (i < strip + EDGE) & (j >= lane) & (j < lane + EDGE)
            total += jnp.where(hit, taps(gap + (i - strip) - (j - lane)), 0.0)
    put_terms(col_ext, total)


def terms(x):
    high = x.astype(BF)
    return high, (x - high.astype(F32)).astype(BF)


def dot(a, b):
    return jnp.dot(a, b, preferred_element_type=F32)


def lanes_of(shape):
    return lax.broadcasted_iota(jnp.int32, shape, 1)


def place(x, source, target, lane):
    moved = pltpu.roll(x, (target - source) % 128, 1) if source != target else x
    return jnp.where((lane >= target) & (lane < target + EDGE), moved, 0.0)


def turned(packed):
    return jnp.transpose(
        jnp.concatenate([packed, jnp.zeros((STRIP - ROWS, 128), F32)], axis=0)
    )


def stack(ref, at, flat):
    rows = flat.shape[0]
    for t in range(STRIP // 128):
        ref[at + rows * t : at + rows * (t + 1)] = flat[:, 128 * t : 128 * t + 128]


def unstack(turn, to, ref, at, rows):
    for t in range(STRIP // 128):
        turn[to : to + rows, 128 * t : 128 * t + 128] = ref[at + rows * t : at + rows * (t + 1)]


def pack_body(ctl, wd, bm, head_dn, head_up, rest_dn, rest_up, sems):
    copies = []

    def copy(source, target):
        copies.append(pltpu.make_async_copy(source, target, sems.at[len(copies)]))
        copies[-1].start()

    for down in (True, False):
        rows = pl.ds(CY - REACH if down else 0, REACH)
        for f in range(F):
            out = (head_dn if down else head_up) if f < HEAD else (rest_dn if down else rest_up)
            copy(ctl.at[f, rows], out.at[pl.ds((f if f < HEAD else f - HEAD) * REACH, REACH)])
        out = rest_dn if down else rest_up
        for k, ref in enumerate((wd, bm)):
            copy(
                ref.at[pl.ds(CY - EXT if down else 0, EXT)],
                out.at[pl.ds((F - HEAD) * REACH + EXT * k, EXT)],
            )
    for done in copies:
        done.wait()


def parcel_body(obs, kind, live, out):
    owners, slots = obs.shape[0], obs.shape[1]
    rows = jnp.concatenate(
        [
            kind[...].astype(F32),
            jnp.broadcast_to(live[...].astype(F32), (slots, owners)),
            jnp.zeros((BLK - 2 * slots, owners), F32),
        ],
        axis=0,
    )
    for q in range(owners):
        out[(slots + 1) * q : (slots + 1) * q + slots] = obs[q]
    out[pl.ds(slots, owners, stride=slots + 1)] = jnp.transpose(rows)


def row_products(pieces, table, tile, put):
    m_high, m_low = table[0], table[1]
    for pair, columns in enumerate(pieces):
        high, low = terms(jnp.concatenate(columns, axis=1))
        size = tile + 2 * HALF
        for at in range(0, high.shape[0] - size + 1, tile):
            xh, xl = high[at : at + size], low[at : at + size]
            put(pair, at, dot(m_high, xh) + (dot(m_high, xl) + dot(m_low, xh)))


def tall_pairs(ctl, first, count, up, dn):
    for f in range(0, count, 2):
        yield [
            jnp.concatenate(
                [up[k * REACH : (k + 1) * REACH], ctl[first + k], dn[k * REACH : (k + 1) * REACH]],
                axis=0,
            )
            for k in (f, f + 1)
        ]


def row_head_body(ctl, up, dn, table, y):
    def put(pair, at, out):
        for k in range(2):
            to = (2 * pair + k) * ROWS + at
            y[to : to + 176] = out[:, 128 * k : 128 * k + 128]

    row_products(tall_pairs(ctl, 0, HEAD, up, dn), table, 176, put)


def row_rest_body(
    ctl, up, dn, wd_hbm, bm_hbm, head, table, to_left, to_right, sa, sb, wd, bm, sems
):
    loads = [
        pltpu.make_async_copy(wd_hbm, wd, sems.at[0]),
        pltpu.make_async_copy(bm_hbm, bm, sems.at[1]),
    ]
    for load in loads:
        load.start()

    def put(pair, at, out):
        for k in range(2):
            to = (2 * pair + k) * ROWS + at
            half = out[:, 128 * k : 128 * k + 128]
            to_left[to : to + 176] = half
            to_right[to : to + 176] = half

    rest = F - HEAD
    row_products(tall_pairs(ctl, HEAD, rest, up, dn), table, 176, put)
    lane = lanes_of((ROWS, 128))
    packed = jnp.zeros((ROWS, 128), F32)
    for f in range(F):
        ref, at = (head, f * ROWS) if f < HEAD else (to_left, (f - HEAD) * ROWS)
        x = ref[at : at + ROWS]
        packed += place(x, 0, EDGE * f, lane) + place(x, CX - EDGE, 32 + EDGE * f, lane)
    for load in loads:
        load.wait()
    for k, own in enumerate((wd, bm)):
        at = rest * REACH + EXT * k
        x = jnp.concatenate([up[at : at + EXT], own[...], dn[at : at + EXT]], axis=0)
        packed += place(x, 0, 64 + EDGE * k, lane) + place(x, CX - EDGE, 80 + EDGE * k, lane)
    flat = turned(packed)
    sa[...] = flat[0:32]
    sb[...] = flat[32:64]
    stack(to_left, rest * ROWS, flat[64:80])
    stack(to_right, rest * ROWS, flat[80:96])


def observe_body(values, foot, out):
    slots, owners = foot.shape
    meta = jnp.transpose(values[pl.ds(slots, owners, stride=slots + 1)])
    slot = lax.broadcasted_iota(jnp.int32, (slots, owners), 0).astype(F32)
    kind = jnp.where(meta[:slots] == 0.0, 0, CY)
    index = jnp.where(slot < meta[slots : 2 * slots], kind + foot[...], -1)
    at = jnp.concatenate([index[k : k + 1] for k in range(slots)], axis=1)
    obs = jnp.concatenate(
        [values[pl.ds(k, owners, stride=slots + 1)] for k in range(slots)], axis=0
    )
    high, low = terms(obs)
    last = (obs - high.astype(F32) - low.astype(F32)).astype(BF)
    first_pair = jnp.concatenate([high, low], axis=1)
    second_pair = jnp.concatenate([last, jnp.ones_like(last)], axis=1)
    for block in range(2 * CY // 128):
        row = lax.broadcasted_iota(jnp.int32, (128, slots * owners), 0) + 128 * block
        hot = jnp.where(row == at, 1.0, 0.0).astype(BF)
        one = dot(hot, first_pair)
        two = dot(hot, second_pair)
        out[128 * block : 128 * block + 128, :128] = one[:, :128] + (one[:, 128:] + two[:, :128])
        out[128 * block : 128 * block + 128, 128:] = two[:, 128:]


def product(x, table):
    xh, xl = terms(x)
    return dot(xh, table[0]) + (dot(xl, table[0]) + dot(xh, table[1]))


def early_body(head, left_head, right_head, rest, table, out):
    sides, own = table[:, : 2 * CX], table[:, 2 * CX :]
    for f in range(F):
        rows = slice(f * ROWS, (f + 1) * ROWS)
        if f < HEAD:
            near = jnp.concatenate([left_head[rows], right_head[rows]], axis=1)
            out[rows] = product(head[rows], own) + product(near, sides)
        else:
            out[rows] = product(rest[(f - HEAD) * ROWS : (f - HEAD + 1) * ROWS], own)


def middle_body(
    spot, scale, early, west_hbm, east_hbm, l2, r2, up, dn, wd, bm, tally, prec, table, ext_table,
    to_head, to_left, to_right, ext, ext_left, ext_right,
    h, u, v, b, p1, p2, q1, q2, e, gw, gb, wdx, bmx, mask, turn, left, right, sems,
):
    started = []

    def load(source, target):
        started.append(pltpu.make_async_copy(source, target, sems.at[len(started)]))
        started[-1].start()
        return started[-1]

    rest = F - HEAD
    tail = pl.ds(rest * ROWS, left.shape[0] - rest * ROWS)
    tails = [load(west_hbm.at[tail], left.at[tail]), load(east_hbm.at[tail], right.at[tail])]
    fields = []
    for f, ref in enumerate((h, u, v, b, p1, p2)):
        waits = [load(early.at[pl.ds(f * ROWS, ROWS)], ref.at[pl.ds(8, ROWS)])]
        if f >= HEAD:
            rows = pl.ds((f - HEAD) * ROWS, ROWS)
            waits.append(load(west_hbm.at[rows], left.at[rows]))
            waits.append(load(east_hbm.at[rows], right.at[rows]))
        fields.append(waits)
        if f == 1:
            inner = (pl.ds(16, CY), pl.ds(0, CX))
            grids = [load(wd, wdx.at[inner]), load(bm, bmx.at[inner])]
    gx, gy, nx, ny = spot[0], spot[1], spot[2], spot[3]
    lane = lanes_of((ROWS, 128))
    turn[0:32] = l2[...]
    turn[32:64] = r2[...]
    for wait in tails:
        wait.wait()
    unstack(turn, 64, left, (F - HEAD) * ROWS, 16)
    unstack(turn, 80, right, (F - HEAD) * ROWS, 16)
    turn[96:128] = jnp.zeros((32, STRIP), F32)
    strips = jnp.transpose(turn[...])[:ROWS]
    edge = jnp.zeros((8, WIDE), F32)
    for ref in (q1, q2, e, gw, gb, mask):
        ref[0:8] = edge
        ref[TALL - 8 : TALL] = edge
    row = lax.broadcasted_iota(jnp.int32, (ROWS, WIDE), 0) - EXT
    wide_lane = lanes_of((ROWS, WIDE))
    column = jnp.where(wide_lane < WIDE * 3 // 4, wide_lane, wide_lane - WIDE)
    row += gy * CY
    column += gx * CX
    inside = (row >= 0) & (row < ny * CY) & (column >= 0) & (column < nx * CX)
    inside_f = jnp.where(inside, 1.0, 0.0)
    mask[8 : 8 + ROWS] = inside_f
    sides = table[:, : 2 * CX]
    far = product(strips, ext_table)
    for f, ref in enumerate((h, u, v, b, p1, p2)):
        if f == 2:
            for k, (wait, grid) in enumerate(zip(grids, (wdx, bmx))):
                wait.wait()
                at = (F - HEAD) * REACH + EXT * k
                grid[0:8] = edge
                grid[TALL - 8 : TALL] = edge
                grid[8:16, :128] = up[at : at + EXT]
                grid[16 + CY : 16 + CY + EXT, :128] = dn[at : at + EXT]
                grid[8 : 8 + ROWS, 128:] = place(strips, 80 + EDGE * k, 0, lane) + place(
                    strips, 64 + EDGE * k, 128 - EDGE, lane
                )
        for wait in fields[f]:
            wait.wait()
        ref[0:8] = edge
        ref[TALL - 8 : TALL] = edge
        out = ref[8 : 8 + ROWS]
        if f >= HEAD:
            rows = slice((f - HEAD) * ROWS, (f - HEAD + 1) * ROWS)
            out += product(jnp.concatenate([left[rows], right[rows]], axis=1), sides)
        edges = place(far, 8 * f, 128 - EDGE, lane) + place(far, 64 + 8 * f, 0, lane)
        out = jnp.concatenate([out[:, :128], out[:, 128:] + edges], axis=1) * scale[f]
        ref[8 : 8 + ROWS] = out * inside_f if f >= 4 else out
        if f == 2:
            gw[8 : 8 + ROWS] = wdx[8 : 8 + ROWS] * out
            gb[8 : 8 + ROWS] = bmx[8 : 8 + ROWS] * out

    def east_west(x):
        return pltpu.roll(x, WIDE - 1, 1), pltpu.roll(x, 1, 1)

    def slope_x(x):
        east, west = east_west(x)
        return east - west

    def at(ref, i, by=0):
        view = ref.at[pl.ds(pl.multiple_of(i * CHUNK, 8), CHUNK + 16)]
        return view[8 + by : 8 + by + CHUNK]

    def put(ref, i, value):
        ref[pl.ds(pl.multiple_of(i * CHUNK + 8, 8), CHUNK)] = value

    def slope_y(ref, i):
        return at(ref, i, 1) - at(ref, i, -1)

    def around(ref, i, centre):
        east, west = east_west(centre)
        return (at(ref, i, 1) + at(ref, i, -1)) + (east + west)

    def sweep(body):
        def step(i, carry):
            body(i)
            return carry

        lax.fori_loop(0, ROWS // CHUNK, step, 0)

    def levels(s1, s2, s1_new, s2_new):
        def body(i):
            uc = at(u, i)
            c1, c2 = at(s1, i), at(s2, i)
            hn = at(h, i) - HALF_DT * (slope_x(at(wdx, i) * uc) + slope_y(gw, i))
            bn = (
                at(b, i)
                - HALF_DT * (slope_x(at(bmx, i) * uc) + slope_y(gb, i))
                + (DT * WS[0]) * c1
                + (DT * WS[1]) * c2
            )
            put(h, i, hn)
            put(b, i, bn)
            if s1_new is not None:
                m = at(mask, i)
                put(e, i, m * (hn + bn))
                for k, (old, c, ref) in enumerate(((s1, c1, s1_new), (s2, c2, s2_new))):
                    keep = 1.0 - DT * WS[k] - 4.0 * DT * NU[k]
                    put(ref, i, m * (keep * c + (DT * NU[k]) * around(old, i, c)))

        sweep(body)

    def speeds():
        def body(i):
            put(u, i, DECAY * at(u, i) - HALF_DT * slope_x(at(e, i)))
            vn = DECAY * at(v, i) - HALF_DT * slope_y(e, i)
            put(v, i, vn)
            put(gw, i, at(wdx, i) * vn)
            put(gb, i, at(bmx, i) * vn)

        sweep(body)

    levels(p1, p2, q1, q2)
    speeds()
    levels(q1, q2, p1, p2)
    speeds()
    levels(p1, p2, None, None)

    bed = b[16 : 16 + CY, :128]
    surface = h[16 : 16 + CY, :128] + bed
    sens = []
    for k, field in enumerate((surface, bed)):
        sums = tally[k * CY : (k + 1) * CY, :128]
        count = tally[k * CY : (k + 1) * CY, 128:]
        mh, ml = terms(count * field - sums)
        rh, rl = terms(prec[k])
        sens.append(dot(mh, rh) + (dot(ml, rh) + dot(mh, rl)))
    for ref, value in ((h, sens[0]), (b, sens[0] + sens[1])):
        ref[8:16] = edge
        ref[16 + CY : 16 + CY + EXT] = edge
        ref[16 : 16 + CY, 128:] = jnp.zeros((CY, 128), F32)
        ref[16 : 16 + CY, :128] = value

    def lift():
        def body(i):
            m = at(mask, i)
            surf = (HALF_DT * m) * (slope_x(at(u, i)) + slope_y(v, i))
            put(h, i, at(h, i) + surf)
            put(b, i, at(b, i) + surf)

        sweep(body)

    def back(s1, s2, s1_new, s2_new):
        def body(i):
            hc, bc = at(h, i), at(b, i)
            depth, mobile = HALF_DT * at(wdx, i), HALF_DT * at(bmx, i)
            un = depth * slope_x(hc) + mobile * slope_x(bc)
            vn = depth * slope_y(h, i) + mobile * slope_y(b, i)
            m = at(mask, i)
            if s1 is None:
                put(u, i, un)
                put(v, i, vn)
                put(s1_new, i, (DT * WS[0]) * bc)
                put(s2_new, i, (DT * WS[1]) * bc)
            else:
                put(u, i, DECAY * at(u, i) + un)
                put(v, i, DECAY * at(v, i) + vn)
                for k, (old, new) in enumerate(((s1, s1_new), (s2, s2_new))):
                    c = at(old, i)
                    keep = 1.0 - DT * WS[k] - 4.0 * DT * NU[k]
                    put(
                        new,
                        i,
                        m * (keep * c + (DT * NU[k]) * around(old, i, c) + (DT * WS[k]) * bc),
                    )

        sweep(body)

    back(None, None, p1, p2)
    lift()
    back(p1, p2, q1, q2)
    lift()
    back(q1, q2, p1, p2)

    packed = jnp.zeros((ROWS, 128), F32)
    for f, ref in enumerate((h, u, v, b, p1, p2)):
        x = ref[8 : 8 + ROWS, :128] * scale[f]
        if f < HEAD:
            to_head[f * ROWS : (f + 1) * ROWS] = x
        else:
            to_left[(f - HEAD) * ROWS : (f - HEAD + 1) * ROWS] = x
            to_right[(f - HEAD) * ROWS : (f - HEAD + 1) * ROWS] = x
        x = ref[8 : 8 + ROWS, 128:] * scale[f]
        packed += place(x, 128 - EDGE, EDGE * f, lane) + place(x, 0, 32 + EDGE * f, lane)
    ext[...] = packed
    flat = turned(packed)
    ext_left[...] = flat[0:32]
    ext_right[...] = flat[32:64]
    stack(to_left, (F - HEAD) * ROWS, flat[0:32])
    stack(to_right, (F - HEAD) * ROWS, flat[32:64])


def column_back(fields, first, own, left, right, mine, near, far, table, z, to_up, to_dn):
    lane = lanes_of((ROWS, 128))
    th, tl = table[0], table[1]
    for k in range(fields):
        at = slice(k * ROWS, (k + 1) * ROWS)
        one, two = EDGE * (first + k), 32 + EDGE * (first + k)
        west = left[at] + (place(far, one, 0, lane) + place(mine, one, CX - EDGE, lane))
        here = own[at] + (place(near, one, 0, lane) + place(near, two, CX - EDGE, lane))
        east = right[at] + (place(mine, two, 0, lane) + place(far, two, CX - EDGE, lane))
        xh, xl = terms(jnp.concatenate([west, here, east], axis=1))
        out = dot(xh, th) + (dot(xl, th) + dot(xh, tl))
        z[k] = out
        to_up[k] = out[:REACH]
        to_dn[k] = out[ROWS - REACH :]


def column_rest_body(
    own, ext, left, right, l2, r2, table, z, to_up, to_dn, near_out, far_out, turn
):
    turn[64:128] = jnp.zeros((64, STRIP), F32)
    unstack(turn, 0, left, (F - HEAD) * ROWS, 32)
    unstack(turn, 32, right, (F - HEAD) * ROWS, 32)
    near = jnp.transpose(turn[...])[:ROWS]
    turn[0:32] = l2[...]
    turn[32:64] = r2[...]
    far = jnp.transpose(turn[...])[:ROWS]
    near_out[...] = near
    far_out[...] = far
    column_back(F - HEAD, HEAD, own, left, right, ext[...], near, far, table, z, to_up, to_dn)


def column_head_body(own, ext, left, right, near, far, table, z, to_up, to_dn):
    column_back(HEAD, 0, own, left, right, ext[...], near[...], far[...], table, z, to_up, to_dn)


def row_back_body(z_head, up_head, dn_head, z_rest, up_rest, dn_rest, ctl, table, out):
    def pairs():
        for f in range(0, F, 2):
            columns = []
            for k in (f, f + 1):
                z, up, dn, at = (
                    (z_head, up_head, dn_head, k)
                    if k < HEAD
                    else (z_rest, up_rest, dn_rest, k - HEAD)
                )
                columns.append(
                    jnp.concatenate(
                        [
                            up[at, : HALF - EXT],
                            up[at, HALF - EXT :] + z[at, : 2 * EXT],
                            z[at, 2 * EXT : ROWS - 2 * EXT],
                            z[at, ROWS - 2 * EXT :] + dn[at, : 2 * EXT],
                            dn[at, 2 * EXT :],
                        ],
                        axis=0,
                    )
                )
            yield columns

    def put(pair, at, res):
        for k in range(2):
            f = 2 * pair + k
            out[f, at : at + 256] = ctl[f, at : at + 256] + res[:, 128 * k : 128 * k + 128]

    row_products(pairs(), table, 256, put)


def call(body, outs, n_in, scratch=(), smem=0, mib=16, hbm=()):
    specs = [pl.BlockSpec(memory_space=pltpu.SMEM)] * smem
    specs += [
        pl.BlockSpec(memory_space=pltpu.HBM if i in hbm else pltpu.VMEM)
        for i in range(smem, n_in)
    ]
    run = pl.pallas_call(
        body,
        out_shape=[s if hasattr(s, "dtype") else jax.ShapeDtypeStruct(s, F32) for s in outs],
        in_specs=specs,
        out_specs=[pl.BlockSpec(memory_space=pltpu.VMEM)] * len(outs),
        scratch_shapes=list(scratch),
        compiler_params=pltpu.CompilerParams(vmem_limit_bytes=mib << 20),
    )

    def apply(*args):
        return run(
            *(
                pltpu.with_memory_space_constraint(x, pltpu.HBM) if i in hbm else x
                for i, x in enumerate(args)
            )
        )

    return apply


def send(x, axis, by):
    count = lax.axis_size(axis)
    return lax.ppermute(x, axis, [(i, i + by) for i in range(count) if 0 <= i + by < count])


def on_device(
    control, field_scale, water_depth, bed_mobility, footprint, instrument, live_counts,
    observed, obs_precision,
):
    dma = pltpu.SemaphoreType.DMA
    rest_rows = (F - HEAD) * REACH + 2 * EXT
    head_dn, head_up, rest_dn, rest_up = call(
        pack_body,
        [(HEAD * REACH, CX)] * 2 + [(rest_rows, CX)] * 2,
        3,
        [dma((2 * (F + 2),))],
        mib=3,
        hbm=(0, 1, 2),
    )(control, water_depth, bed_mobility)
    up_head = send(head_dn, GY, 1)
    dn_head = send(head_up, GY, -1)
    up_rest = send(rest_dn, GY, 1)
    dn_rest = send(rest_up, GY, -1)

    def table(*shape):
        return jax.ShapeDtypeStruct((2,) + shape, BF)

    (row_fwd,) = call(row_table_body, [table(176, 432)], 0, mib=2)()
    row_bwd, col_fwd, col_ext, col_bwd = call(
        table_body,
        [table(256, 512), table(3 * CX, WIDE), table(CX, CX), table(3 * CX, CX)],
        0,
        mib=6,
    )()

    owners, slots = instrument.shape[1:]
    lots = owners * (slots + 1)
    (parcel,) = call(parcel_body, [(lots, BLK)], 3, mib=3)(
        observed[0], jnp.swapaxes(instrument[0], 0, 1), live_counts
    )
    received = lax.all_to_all(
        parcel.reshape(owners, 1, (slots + 1) * BLK),
        (GX, GY),
        split_axis=0,
        concat_axis=0,
        tiled=True,
    ).reshape(lots, BLK)
    (tally,) = call(observe_body, [(2 * CY, 2 * BLK)], 2, mib=8)(
        received, jnp.swapaxes(footprint[0], 0, 1)
    )

    rest = F - HEAD
    (head,) = call(row_head_body, [(HEAD * ROWS, CX)], 4, mib=8)(control, up_head, dn_head, row_fwd)
    left_head = send(head, GX, 1)
    right_head = send(head, GX, -1)
    big = rest * ROWS + 16 * STRIP // 128
    y, y_right, sa, sb = call(
        row_rest_body,
        [(big, CX), (big, CX), (32, STRIP), (32, STRIP)],
        7,
        [pltpu.VMEM((CY, CX), F32)] * 2 + [dma((2,))],
        hbm=(3, 4),
    )(control, up_rest, dn_rest, water_depth, bed_mobility, head, row_fwd)
    l2 = send(sb, GX, 2)
    r2 = send(sa, GX, -2)
    left = send(y_right, GX, 1)
    right = send(y, GX, -1)

    spot = jnp.stack(
        [
            lax.axis_index(GX),
            lax.axis_index(GY),
            lax.axis_size(GX),
            lax.axis_size(GY),
        ]
    ).astype(jnp.int32)
    near_rows = big
    (early,) = call(early_body, [(F * ROWS, WIDE)], 5)(head, left_head, right_head, y, col_fwd)
    big = rest * ROWS + 32 * STRIP // 128
    main_head, main, main_right, ext, ext_left, ext_right = call(
        middle_body,
        [
            (HEAD * ROWS, CX), (big, CX), (big, CX), (ROWS, CX), (32, STRIP), (32, STRIP),
        ],
        15,
        [pltpu.VMEM((TALL, WIDE), F32)] * 14 + [pltpu.VMEM((128, STRIP), F32)] + [pltpu.VMEM((near_rows, CX), F32)] * 2 + [dma((18,))],
        smem=2,
        mib=MID,
        hbm=(2, 3, 4, 9, 10),
    )(
        spot, field_scale, early, left, right, l2, r2,
        up_rest, dn_rest, water_depth, bed_mobility, tally, obs_precision, col_fwd, col_ext,
    )

    l2 = send(ext_right, GX, 2)
    r2 = send(ext_left, GX, -2)
    left = send(main_right, GX, 1)
    right = send(main, GX, -1)
    left_head = send(main_head, GX, 1)
    right_head = send(main_head, GX, -1)
    z_rest, to_up, to_dn, near, far = call(
        column_rest_body,
        [(rest, ROWS, CX), (rest, REACH, CX), (rest, REACH, CX), (ROWS, CX), (ROWS, CX)],
        7,
        [pltpu.VMEM((128, STRIP), F32)],
    )(main, ext, left, right, l2, r2, col_bwd)
    up_rest, dn_rest = send(to_dn, GY, 1), send(to_up, GY, -1)
    z_head, to_up, to_dn = call(
        column_head_body, [(HEAD, ROWS, CX), (HEAD, REACH, CX), (HEAD, REACH, CX)], 7
    )(main_head, ext, left_head, right_head, near, far, col_bwd)
    up_head, dn_head = send(to_dn, GY, 1), send(to_up, GY, -1)
    (out,) = call(row_back_body, [(F, CY, CX)], 8)(
        z_head, up_head, dn_head, z_rest, up_rest, dn_rest, control, row_bwd
    )
    return out


def solution(mesh):
    in_specs = (
        P(None, GY, GX),
        P(),
        P(GY, GX),
        P(GY, GX),
        P((GX, GY), None, None),
        P((GX, GY), None, None),
        P((GX, GY), None),
        P((GX, GY), None, None, None),
        P(),
    )
    return jax.shard_map(
        on_device, mesh=mesh, in_specs=in_specs, out_specs=P(None, GY, GX), check_vma=False
    )
```

```python
import math

import jax
import jax.numpy as jnp
import numpy as np
from jax import lax
from jax.experimental import pallas as pl
from jax.experimental.pallas import tpu as pltpu
from jax.sharding import PartitionSpec as P


HALF = 128
BLK = 128
F = 6
CX = 128
CY = 512
EXT = 8
REACH = HALF + EXT
ROWS = CY + 2 * EXT
TALL = ROWS + 16
WIDE = 256
EDGE = 5
STRIP = 640
HEAD = 2
CHUNK = ROWS

DT = 0.2
DECAY = 1.0 - DT * 0.5
HALF_DT = 0.5 * DT
NU = (0.4, 0.25)
WS = (0.5, 0.2)


GX, GY = "gx", "gy"
MID = 20
BF = jnp.bfloat16
F32 = jnp.float32


def norm():
    steps = np.arange(-HALF, HALF + 1, dtype=np.float64)
    return math.sqrt(np.sum(np.exp(-steps * steps / (HALF / 2.0) ** 2)))


def taps(offset):
    far = offset.astype(F32)
    value = jnp.exp(far * far * (-0.5 / (HALF / 2.0) ** 2)) * (1.0 / norm())
    return jnp.where(jnp.abs(offset) <= HALF, value, 0.0)


def axes(shape):
    return [lax.broadcasted_iota(jnp.int32, shape, d) for d in range(2)]


def put_terms(ref, value):
    high, low = terms(value)
    ref[0] = high
    ref[1] = low


def row_table_body(ref):
    i, j = axes(ref.shape[1:])
    put_terms(ref, taps(j - HALF - i))


def table_body(row_bwd, col_fwd, col_ext, col_bwd):
    row_table_body(row_bwd)
    i, j = axes(col_bwd.shape[1:])
    put_terms(col_bwd, taps(i - CX - j))
    i, j = axes((3 * CX, WIDE))
    column = jnp.where(j < WIDE * 3 // 4, j, j - WIDE)
    used = (j < CX + EDGE) | (j >= WIDE - EDGE)
    source = jnp.where(i < CX, i - CX, jnp.where(i < 2 * CX, i, i - 2 * CX))
    put_terms(col_fwd, jnp.where(used, taps(source - column), 0.0))
    i, j = axes((CX, CX))
    total = jnp.zeros((CX, CX), F32)
    for f in range(F):
        for strip, lane, gap in ((EDGE * f, 8 * f, -CX), (32 + EDGE * f, 64 + 8 * f, CX)):
            hit = (i >= strip) & (i < strip + EDGE) & (j >= lane) & (j < lane + EDGE)
            total += jnp.where(hit, taps(gap + (i - strip) - (j - lane)), 0.0)
    put_terms(col_ext, total)


def terms(x):
    high = x.astype(BF)
    return high, (x - high.astype(F32)).astype(BF)


def dot(a, b):
    return jnp.dot(a, b, preferred_element_type=F32)


def lanes_of(shape):
    return lax.broadcasted_iota(jnp.int32, shape, 1)


def place(x, source, target, lane):
    moved = pltpu.roll(x, (target - source) % 128, 1) if source != target else x
    return jnp.where((lane >= target) & (lane < target + EDGE), moved, 0.0)


def turned(packed):
    return jnp.transpose(
        jnp.concatenate([packed, jnp.zeros((STRIP - ROWS, 128), F32)], axis=0)
    )


def stack(ref, at, flat):
    rows = flat.shape[0]
    for t in range(STRIP // 128):
        ref[at + rows * t : at + rows * (t + 1)] = flat[:, 128 * t : 128 * t + 128]


def unstack(turn, to, ref, at, rows):
    for t in range(STRIP // 128):
        turn[to : to + rows, 128 * t : 128 * t + 128] = ref[at + rows * t : at + rows * (t + 1)]


def pack_body(ctl, wd, bm, head_dn, head_up, rest_dn, rest_up, sems):
    copies = []

    def copy(source, target):
        copies.append(pltpu.make_async_copy(source, target, sems.at[len(copies)]))
        copies[-1].start()

    for down in (True, False):
        rows = pl.ds(CY - REACH if down else 0, REACH)
        for f in range(F):
            out = (head_dn if down else head_up) if f < HEAD else (rest_dn if down else rest_up)
            copy(ctl.at[f, rows], out.at[pl.ds((f if f < HEAD else f - HEAD) * REACH, REACH)])
        out = rest_dn if down else rest_up
        for k, ref in enumerate((wd, bm)):
            copy(
                ref.at[pl.ds(CY - EXT if down else 0, EXT)],
                out.at[pl.ds((F - HEAD) * REACH + EXT * k, EXT)],
            )
    for done in copies:
        done.wait()


def parcel_body(obs, kind, live, out):
    owners, slots = obs.shape[0], obs.shape[1]
    rows = jnp.concatenate(
        [
            kind[...].astype(F32),
            jnp.broadcast_to(live[...].astype(F32), (slots, owners)),
            jnp.zeros((BLK - 2 * slots, owners), F32),
        ],
        axis=0,
    )
    for q in range(owners):
        out[(slots + 1) * q : (slots + 1) * q + slots] = obs[q]
    out[pl.ds(slots, owners, stride=slots + 1)] = jnp.transpose(rows)


def row_products(pieces, table, tile, put):
    m_high, m_low = table[0], table[1]
    for pair, columns in enumerate(pieces):
        high, low = terms(jnp.concatenate(columns, axis=1))
        size = tile + 2 * HALF
        for at in range(0, high.shape[0] - size + 1, tile):
            xh, xl = high[at : at + size], low[at : at + size]
            put(pair, at, dot(m_high, xh) + (dot(m_high, xl) + dot(m_low, xh)))


def tall_pairs(ctl, first, count, up, dn):
    for f in range(0, count, 2):
        yield [
            jnp.concatenate(
                [up[k * REACH : (k + 1) * REACH], ctl[first + k], dn[k * REACH : (k + 1) * REACH]],
                axis=0,
            )
            for k in (f, f + 1)
        ]


def row_head_body(ctl, up, dn, table, y):
    def put(pair, at, out):
        for k in range(2):
            to = (2 * pair + k) * ROWS + at
            y[to : to + 176] = out[:, 128 * k : 128 * k + 128]

    row_products(tall_pairs(ctl, 0, HEAD, up, dn), table, 176, put)


def row_rest_body(
    ctl, up, dn, wd_hbm, bm_hbm, head, table, to_left, to_right, sa, sb, wd, bm, sems
):
    loads = [
        pltpu.make_async_copy(wd_hbm, wd, sems.at[0]),
        pltpu.make_async_copy(bm_hbm, bm, sems.at[1]),
    ]
    for load in loads:
        load.start()

    def put(pair, at, out):
        for k in range(2):
            to = (2 * pair + k) * ROWS + at
            half = out[:, 128 * k : 128 * k + 128]
            to_left[to : to + 176] = half
            to_right[to : to + 176] = half

    rest = F - HEAD
    row_products(tall_pairs(ctl, HEAD, rest, up, dn), table, 176, put)
    lane = lanes_of((ROWS, 128))
    packed = jnp.zeros((ROWS, 128), F32)
    for f in range(F):
        ref, at = (head, f * ROWS) if f < HEAD else (to_left, (f - HEAD) * ROWS)
        x = ref[at : at + ROWS]
        packed += place(x, 0, EDGE * f, lane) + place(x, CX - EDGE, 32 + EDGE * f, lane)
    for load in loads:
        load.wait()
    for k, own in enumerate((wd, bm)):
        at = rest * REACH + EXT * k
        x = jnp.concatenate([up[at : at + EXT], own[...], dn[at : at + EXT]], axis=0)
        packed += place(x, 0, 64 + EDGE * k, lane) + place(x, CX - EDGE, 80 + EDGE * k, lane)
    flat = turned(packed)
    sa[...] = flat[0:32]
    sb[...] = flat[32:64]
    stack(to_left, rest * ROWS, flat[64:80])
    stack(to_right, rest * ROWS, flat[80:96])


def observe_body(values, foot, out):
    slots, owners = foot.shape
    meta = jnp.transpose(values[pl.ds(slots, owners, stride=slots + 1)])
    slot = lax.broadcasted_iota(jnp.int32, (slots, owners), 0).astype(F32)
    kind = jnp.where(meta[:slots] == 0.0, 0, CY)
    index = jnp.where(slot < meta[slots : 2 * slots], kind + foot[...], -1)
    at = jnp.concatenate([index[k : k + 1] for k in range(slots)], axis=1)
    obs = jnp.concatenate(
        [values[pl.ds(k, owners, stride=slots + 1)] for k in range(slots)], axis=0
    )
    high, low = terms(obs)
    last = (obs - high.astype(F32) - low.astype(F32)).astype(BF)
    first_pair = jnp.concatenate([high, low], axis=1)
    second_pair = jnp.concatenate([last, jnp.ones_like(last)], axis=1)
    for block in range(2 * CY // 128):
        row = lax.broadcasted_iota(jnp.int32, (128, slots * owners), 0) + 128 * block
        hot = jnp.where(row == at, 1.0, 0.0).astype(BF)
        one = dot(hot, first_pair)
        two = dot(hot, second_pair)
        out[128 * block : 128 * block + 128, :128] = one[:, :128] + (one[:, 128:] + two[:, :128])
        out[128 * block : 128 * block + 128, 128:] = two[:, 128:]


def product(x, table):
    xh, xl = terms(x)
    return dot(xh, table[0]) + (dot(xl, table[0]) + dot(xh, table[1]))


def early_body(head, left_head, right_head, rest, table, after, out):
    sides, own = table[:, : 2 * CX], table[:, 2 * CX :]
    for f in range(F):
        rows = slice(f * ROWS, (f + 1) * ROWS)
        if f < HEAD:
            near = jnp.concatenate([left_head[rows], right_head[rows]], axis=1)
            out[rows] = product(head[rows], own) + product(near, sides)
        else:
            out[rows] = product(rest[(f - HEAD) * ROWS : (f - HEAD + 1) * ROWS], own)


def middle_body(
    spot, scale, early, west_hbm, east_hbm, l2, r2, up, dn, wd, bm, tally, prec, table, ext_table,
    to_head, to_left, to_right, ext, ext_left, ext_right,
    h, u, v, b, p1, p2, q1, q2, e, gw, gb, wdx, bmx, mask, turn, left, right, sems,
):
    started = []

    def load(source, target):
        started.append(pltpu.make_async_copy(source, target, sems.at[len(started)]))
        started[-1].start()
        return started[-1]

    rest = F - HEAD
    tail = pl.ds(rest * ROWS, left.shape[0] - rest * ROWS)
    tails = [load(west_hbm.at[tail], left.at[tail]), load(east_hbm.at[tail], right.at[tail])]
    fields = []
    for f, ref in enumerate((h, u, v, b, p1, p2)):
        waits = []
        if f >= HEAD:
            rows = pl.ds((f - HEAD) * ROWS, ROWS)
            waits.append(load(west_hbm.at[rows], left.at[rows]))
            waits.append(load(east_hbm.at[rows], right.at[rows]))
        fields.append(waits)
        if f == 1:
            inner = (pl.ds(16, CY), pl.ds(0, CX))
            grids = [load(wd, wdx.at[inner]), load(bm, bmx.at[inner])]
    gx, gy, nx, ny = spot[0], spot[1], spot[2], spot[3]
    lane = lanes_of((ROWS, 128))
    turn[0:32] = l2[...]
    turn[32:64] = r2[...]
    for wait in tails:
        wait.wait()
    unstack(turn, 64, left, (F - HEAD) * ROWS, 16)
    unstack(turn, 80, right, (F - HEAD) * ROWS, 16)
    turn[96:128] = jnp.zeros((32, STRIP), F32)
    strips = jnp.transpose(turn[...])[:ROWS]
    edge = jnp.zeros((8, WIDE), F32)
    for ref in (q1, q2, e, gw, gb, mask):
        ref[0:8] = edge
        ref[TALL - 8 : TALL] = edge
    row = lax.broadcasted_iota(jnp.int32, (ROWS, WIDE), 0) - EXT
    wide_lane = lanes_of((ROWS, WIDE))
    column = jnp.where(wide_lane < WIDE * 3 // 4, wide_lane, wide_lane - WIDE)
    row += gy * CY
    column += gx * CX
    inside = (row >= 0) & (row < ny * CY) & (column >= 0) & (column < nx * CX)
    inside_f = jnp.where(inside, 1.0, 0.0)
    mask[8 : 8 + ROWS] = inside_f
    sides = table[:, : 2 * CX]
    far = product(strips, ext_table)
    for f, ref in enumerate((h, u, v, b, p1, p2)):
        if f == 2:
            for k, (wait, grid) in enumerate(zip(grids, (wdx, bmx))):
                wait.wait()
                at = (F - HEAD) * REACH + EXT * k
                grid[0:8] = edge
                grid[TALL - 8 : TALL] = edge
                grid[8:16, :128] = up[at : at + EXT]
                grid[16 + CY : 16 + CY + EXT, :128] = dn[at : at + EXT]
                grid[8 : 8 + ROWS, 128:] = place(strips, 80 + EDGE * k, 0, lane) + place(
                    strips, 64 + EDGE * k, 128 - EDGE, lane
                )
        for wait in fields[f]:
            wait.wait()
        ref[0:8] = edge
        ref[TALL - 8 : TALL] = edge
        out = early[f * ROWS : (f + 1) * ROWS]
        if f >= HEAD:
            rows = slice((f - HEAD) * ROWS, (f - HEAD + 1) * ROWS)
            out += product(jnp.concatenate([left[rows], right[rows]], axis=1), sides)
        edges = place(far, 8 * f, 128 - EDGE, lane) + place(far, 64 + 8 * f, 0, lane)
        out = jnp.concatenate([out[:, :128], out[:, 128:] + edges], axis=1) * scale[f]
        ref[8 : 8 + ROWS] = out * inside_f if f >= 4 else out
        if f == 2:
            gw[8 : 8 + ROWS] = wdx[8 : 8 + ROWS] * out
            gb[8 : 8 + ROWS] = bmx[8 : 8 + ROWS] * out

    def east_west(x):
        return pltpu.roll(x, WIDE - 1, 1), pltpu.roll(x, 1, 1)

    def slope_x(x):
        east, west = east_west(x)
        return east - west

    def at(ref, i, by=0):
        view = ref.at[pl.ds(pl.multiple_of(i * CHUNK, 8), CHUNK + 16)]
        return view[8 + by : 8 + by + CHUNK]

    def put(ref, i, value):
        ref[pl.ds(pl.multiple_of(i * CHUNK + 8, 8), CHUNK)] = value

    def slope_y(ref, i):
        return at(ref, i, 1) - at(ref, i, -1)

    def around(ref, i, centre):
        east, west = east_west(centre)
        return (at(ref, i, 1) + at(ref, i, -1)) + (east + west)

    def sweep(body):
        def step(i, carry):
            body(i)
            return carry

        lax.fori_loop(0, ROWS // CHUNK, step, 0)

    def levels(s1, s2, s1_new, s2_new):
        def body(i):
            uc = at(u, i)
            c1, c2 = at(s1, i), at(s2, i)
            hn = at(h, i) - HALF_DT * (slope_x(at(wdx, i) * uc) + slope_y(gw, i))
            bn = (
                at(b, i)
                - HALF_DT * (slope_x(at(bmx, i) * uc) + slope_y(gb, i))
                + (DT * WS[0]) * c1
                + (DT * WS[1]) * c2
            )
            put(h, i, hn)
            put(b, i, bn)
            if s1_new is not None:
                m = at(mask, i)
                put(e, i, m * (hn + bn))
                for k, (old, c, ref) in enumerate(((s1, c1, s1_new), (s2, c2, s2_new))):
                    keep = 1.0 - DT * WS[k] - 4.0 * DT * NU[k]
                    put(ref, i, m * (keep * c + (DT * NU[k]) * around(old, i, c)))

        sweep(body)

    def speeds():
        def body(i):
            put(u, i, DECAY * at(u, i) - HALF_DT * slope_x(at(e, i)))
            vn = DECAY * at(v, i) - HALF_DT * slope_y(e, i)
            put(v, i, vn)
            put(gw, i, at(wdx, i) * vn)
            put(gb, i, at(bmx, i) * vn)

        sweep(body)

    levels(p1, p2, q1, q2)
    speeds()
    levels(q1, q2, p1, p2)
    speeds()
    levels(p1, p2, None, None)

    bed = b[16 : 16 + CY, :128]
    surface = h[16 : 16 + CY, :128] + bed
    sens = []
    for k, field in enumerate((surface, bed)):
        sums = tally[k * CY : (k + 1) * CY, :128]
        count = tally[k * CY : (k + 1) * CY, 128:]
        mh, ml = terms(count * field - sums)
        rh, rl = terms(prec[k])
        sens.append(dot(mh, rh) + (dot(ml, rh) + dot(mh, rl)))
    for ref, value in ((h, sens[0]), (b, sens[0] + sens[1])):
        ref[8:16] = edge
        ref[16 + CY : 16 + CY + EXT] = edge
        ref[16 : 16 + CY, 128:] = jnp.zeros((CY, 128), F32)
        ref[16 : 16 + CY, :128] = value

    def lift():
        def body(i):
            m = at(mask, i)
            surf = (HALF_DT * m) * (slope_x(at(u, i)) + slope_y(v, i))
            put(h, i, at(h, i) + surf)
            put(b, i, at(b, i) + surf)

        sweep(body)

    def back(s1, s2, s1_new, s2_new):
        def body(i):
            hc, bc = at(h, i), at(b, i)
            depth, mobile = HALF_DT * at(wdx, i), HALF_DT * at(bmx, i)
            un = depth * slope_x(hc) + mobile * slope_x(bc)
            vn = depth * slope_y(h, i) + mobile * slope_y(b, i)
            m = at(mask, i)
            if s1 is None:
                put(u, i, un)
                put(v, i, vn)
                put(s1_new, i, (DT * WS[0]) * bc)
                put(s2_new, i, (DT * WS[1]) * bc)
            else:
                put(u, i, DECAY * at(u, i) + un)
                put(v, i, DECAY * at(v, i) + vn)
                for k, (old, new) in enumerate(((s1, s1_new), (s2, s2_new))):
                    c = at(old, i)
                    keep = 1.0 - DT * WS[k] - 4.0 * DT * NU[k]
                    put(
                        new,
                        i,
                        m * (keep * c + (DT * NU[k]) * around(old, i, c) + (DT * WS[k]) * bc),
                    )

        sweep(body)

    back(None, None, p1, p2)
    lift()
    back(p1, p2, q1, q2)
    lift()
    back(q1, q2, p1, p2)

    packed = jnp.zeros((ROWS, 128), F32)
    for f, ref in enumerate((h, u, v, b, p1, p2)):
        x = ref[8 : 8 + ROWS, :128] * scale[f]
        if f < HEAD:
            to_head[f * ROWS : (f + 1) * ROWS] = x
        else:
            to_left[(f - HEAD) * ROWS : (f - HEAD + 1) * ROWS] = x
            to_right[(f - HEAD) * ROWS : (f - HEAD + 1) * ROWS] = x
        x = ref[8 : 8 + ROWS, 128:] * scale[f]
        packed += place(x, 128 - EDGE, EDGE * f, lane) + place(x, 0, 32 + EDGE * f, lane)
    ext[...] = packed
    flat = turned(packed)
    ext_left[...] = flat[0:32]
    ext_right[...] = flat[32:64]
    stack(to_left, (F - HEAD) * ROWS, flat[0:32])
    stack(to_right, (F - HEAD) * ROWS, flat[32:64])


def column_back(fields, first, own, left, right, mine, near, far, table, z, to_up, to_dn):
    lane = lanes_of((ROWS, 128))
    th, tl = table[0], table[1]
    for k in range(fields):
        at = slice(k * ROWS, (k + 1) * ROWS)
        one, two = EDGE * (first + k), 32 + EDGE * (first + k)
        west = left[at] + (place(far, one, 0, lane) + place(mine, one, CX - EDGE, lane))
        here = own[at] + (place(near, one, 0, lane) + place(near, two, CX - EDGE, lane))
        east = right[at] + (place(mine, two, 0, lane) + place(far, two, CX - EDGE, lane))
        xh, xl = terms(jnp.concatenate([west, here, east], axis=1))
        out = dot(xh, th) + (dot(xl, th) + dot(xh, tl))
        z[k] = out
        to_up[k] = out[:REACH]
        to_dn[k] = out[ROWS - REACH :]


def column_rest_body(
    own, ext, left, right, l2, r2, table, z, to_up, to_dn, near_out, far_out, turn
):
    turn[64:128] = jnp.zeros((64, STRIP), F32)
    unstack(turn, 0, left, (F - HEAD) * ROWS, 32)
    unstack(turn, 32, right, (F - HEAD) * ROWS, 32)
    near = jnp.transpose(turn[...])[:ROWS]
    turn[0:32] = l2[...]
    turn[32:64] = r2[...]
    far = jnp.transpose(turn[...])[:ROWS]
    near_out[...] = near
    far_out[...] = far
    column_back(F - HEAD, HEAD, own, left, right, ext[...], near, far, table, z, to_up, to_dn)


def column_head_body(own, ext, left, right, near, far, table, z, to_up, to_dn):
    column_back(HEAD, 0, own, left, right, ext[...], near[...], far[...], table, z, to_up, to_dn)


def row_back_body(z_head, up_head, dn_head, z_rest, up_rest, dn_rest, ctl, table, out):
    def pairs():
        for f in range(0, F, 2):
            columns = []
            for k in (f, f + 1):
                z, up, dn, at = (
                    (z_head, up_head, dn_head, k)
                    if k < HEAD
                    else (z_rest, up_rest, dn_rest, k - HEAD)
                )
                columns.append(
                    jnp.concatenate(
                        [
                            up[at, : HALF - EXT],
                            up[at, HALF - EXT :] + z[at, : 2 * EXT],
                            z[at, 2 * EXT : ROWS - 2 * EXT],
                            z[at, ROWS - 2 * EXT :] + dn[at, : 2 * EXT],
                            dn[at, 2 * EXT :],
                        ],
                        axis=0,
                    )
                )
            yield columns

    def put(pair, at, res):
        for k in range(2):
            f = 2 * pair + k
            out[f, at : at + 256] = ctl[f, at : at + 256] + res[:, 128 * k : 128 * k + 128]

    row_products(pairs(), table, 256, put)


def call(body, outs, n_in, scratch=(), smem=0, mib=8, hbm=(), out=pltpu.VMEM):
    specs = [pl.BlockSpec(memory_space=pltpu.SMEM)] * smem
    specs += [
        pl.BlockSpec(memory_space=pltpu.HBM if i in hbm else pltpu.VMEM)
        for i in range(smem, n_in)
    ]
    run = pl.pallas_call(
        body,
        out_shape=[s if hasattr(s, "dtype") else jax.ShapeDtypeStruct(s, F32) for s in outs],
        in_specs=specs,
        out_specs=[pl.BlockSpec(memory_space=out)] * len(outs),
        scratch_shapes=list(scratch),
        compiler_params=pltpu.CompilerParams(vmem_limit_bytes=mib << 20),
    )

    def apply(*args):
        return run(
            *(
                pltpu.with_memory_space_constraint(x, pltpu.HBM) if i in hbm else x
                for i, x in enumerate(args)
            )
        )

    return apply


def send(x, axis, by):
    count = lax.axis_size(axis)
    return lax.ppermute(x, axis, [(i, i + by) for i in range(count) if 0 <= i + by < count])


def on_device(
    control, field_scale, water_depth, bed_mobility, footprint, instrument, live_counts,
    observed, obs_precision,
):
    dma = pltpu.SemaphoreType.DMA
    rest_rows = (F - HEAD) * REACH + 2 * EXT
    head_dn, head_up, rest_dn, rest_up = call(
        pack_body,
        [(HEAD * REACH, CX)] * 2 + [(rest_rows, CX)] * 2,
        3,
        [dma((2 * (F + 2),))],
        mib=3,
        out=pltpu.HBM,
        hbm=(0, 1, 2),
    )(control, water_depth, bed_mobility)
    up_head = send(head_dn, GY, 1)
    dn_head = send(head_up, GY, -1)
    up_rest = send(rest_dn, GY, 1)
    dn_rest = send(rest_up, GY, -1)

    def table(*shape):
        return jax.ShapeDtypeStruct((2,) + shape, BF)

    (row_fwd,) = call(row_table_body, [table(176, 432)], 0, mib=2)()
    row_bwd, col_fwd, col_ext, col_bwd = call(
        table_body,
        [table(256, 512), table(3 * CX, WIDE), table(CX, CX), table(3 * CX, CX)],
        0,
        mib=6,
    )()

    owners, slots = instrument.shape[1:]
    lots = owners * (slots + 1)
    (parcel,) = call(parcel_body, [(lots, BLK)], 3, mib=3)(
        observed[0], jnp.swapaxes(instrument[0], 0, 1), live_counts
    )
    received = lax.all_to_all(
        parcel.reshape(owners, 1, (slots + 1) * BLK),
        (GX, GY),
        split_axis=0,
        concat_axis=0,
        tiled=True,
    ).reshape(lots, BLK)
    (tally,) = call(observe_body, [(2 * CY, 2 * BLK)], 2, mib=8)(
        received, jnp.swapaxes(footprint[0], 0, 1)
    )

    rest = F - HEAD
    (head,) = call(row_head_body, [(HEAD * ROWS, CX)], 4, mib=8)(control, up_head, dn_head, row_fwd)
    left_head = send(head, GX, 1)
    right_head = send(head, GX, -1)
    big = rest * ROWS + 16 * STRIP // 128
    y, y_right, sa, sb = call(
        row_rest_body,
        [(big, CX), (big, CX), (32, STRIP), (32, STRIP)],
        7,
        [pltpu.VMEM((CY, CX), F32)] * 2 + [dma((2,))],
        hbm=(3, 4),
    )(control, up_rest, dn_rest, water_depth, bed_mobility, head, row_fwd)
    l2 = send(sb, GX, 2)
    r2 = send(sa, GX, -2)
    left = send(y_right, GX, 1)
    right = send(y, GX, -1)

    spot = jnp.stack(
        [
            lax.axis_index(GX),
            lax.axis_index(GY),
            lax.axis_size(GX),
            lax.axis_size(GY),
        ]
    ).astype(jnp.int32)
    near_rows = big
    (early,) = call(early_body, [(F * ROWS, WIDE)], 6)(
        head, left_head, right_head, y, col_fwd, tally
    )
    big = rest * ROWS + 32 * STRIP // 128
    main_head, main, main_right, ext, ext_left, ext_right = call(
        middle_body,
        [
            (HEAD * ROWS, CX), (big, CX), (big, CX), (ROWS, CX), (32, STRIP), (32, STRIP),
        ],
        15,
        [pltpu.VMEM((TALL, WIDE), F32)] * 14 + [pltpu.VMEM((128, STRIP), F32)] + [pltpu.VMEM((near_rows, CX), F32)] * 2 + [dma((12,))],
        smem=2,
        mib=MID,
        hbm=(3, 4, 9, 10),
    )(
        spot, field_scale, early, left, right, l2, r2,
        up_rest, dn_rest, water_depth, bed_mobility, tally, obs_precision, col_fwd, col_ext,
    )

    l2 = send(ext_right, GX, 2)
    r2 = send(ext_left, GX, -2)
    left = send(main_right, GX, 1)
    right = send(main, GX, -1)
    left_head = send(main_head, GX, 1)
    right_head = send(main_head, GX, -1)
    z_rest, to_up, to_dn, near, far = call(
        column_rest_body,
        [(rest, ROWS, CX), (rest, REACH, CX), (rest, REACH, CX), (ROWS, CX), (ROWS, CX)],
        7,
        [pltpu.VMEM((128, STRIP), F32)],
    )(main, ext, left, right, l2, r2, col_bwd)
    up_rest, dn_rest = send(to_dn, GY, 1), send(to_up, GY, -1)
    z_head, to_up, to_dn = call(
        column_head_body, [(HEAD, ROWS, CX), (HEAD, REACH, CX), (HEAD, REACH, CX)], 7
    )(main_head, ext, left_head, right_head, near, far, col_bwd)
    up_head, dn_head = send(to_dn, GY, 1), send(to_up, GY, -1)
    (out,) = call(row_back_body, [(F, CY, CX)], 8)(
        z_head, up_head, dn_head, z_rest, up_rest, dn_rest, control, row_bwd
    )
    return out


def solution(mesh):
    in_specs = (
        P(None, GY, GX),
        P(),
        P(GY, GX),
        P(GY, GX),
        P((GX, GY), None, None),
        P((GX, GY), None, None),
        P((GX, GY), None),
        P((GX, GY), None, None, None),
        P(),
    )
    return jax.shard_map(
        on_device, mesh=mesh, in_specs=in_specs, out_specs=P(None, GY, GX), check_vma=False
    )
```

```python
import math

import jax
import jax.numpy as jnp
import numpy as np
from jax import lax
from jax.experimental import pallas as pl
from jax.experimental.pallas import tpu as pltpu
from jax.sharding import PartitionSpec as P


HALF = 128
BLK = 128
F = 6
CX = 128
CY = 512
EXT = 8
REACH = HALF + EXT
ROWS = CY + 2 * EXT
TALL = ROWS + 16
WIDE = 256
EDGE = 5
STRIP = 640
HEAD = 2
CHUNK = ROWS

DT = 0.2
DECAY = 1.0 - DT * 0.5
HALF_DT = 0.5 * DT
NU = (0.4, 0.25)
WS = (0.5, 0.2)


GX, GY = "gx", "gy"
MID = 20
BF = jnp.bfloat16
F32 = jnp.float32


def norm():
    steps = np.arange(-HALF, HALF + 1, dtype=np.float64)
    return math.sqrt(np.sum(np.exp(-steps * steps / (HALF / 2.0) ** 2)))


def taps(offset):
    far = offset.astype(F32)
    value = jnp.exp(far * far * (-0.5 / (HALF / 2.0) ** 2)) * (1.0 / norm())
    return jnp.where(jnp.abs(offset) <= HALF, value, 0.0)


def axes(shape):
    return [lax.broadcasted_iota(jnp.int32, shape, d) for d in range(2)]


def put_terms(ref, value):
    high, low = terms(value)
    ref[0] = high
    ref[1] = low


def row_table_body(ref):
    i, j = axes(ref.shape[1:])
    put_terms(ref, taps(j - HALF - i))


def table_body(row_bwd, col_fwd, col_ext, col_bwd):
    row_table_body(row_bwd)
    i, j = axes(col_bwd.shape[1:])
    put_terms(col_bwd, taps(i - CX - j))
    i, j = axes((3 * CX, WIDE))
    column = jnp.where(j < WIDE * 3 // 4, j, j - WIDE)
    used = (j < CX + EDGE) | (j >= WIDE - EDGE)
    source = jnp.where(i < CX, i - CX, jnp.where(i < 2 * CX, i, i - 2 * CX))
    put_terms(col_fwd, jnp.where(used, taps(source - column), 0.0))
    i, j = axes((CX, CX))
    total = jnp.zeros((CX, CX), F32)
    for f in range(F):
        for strip, lane, gap in ((EDGE * f, 8 * f, -CX), (32 + EDGE * f, 64 + 8 * f, CX)):
            hit = (i >= strip) & (i < strip + EDGE) & (j >= lane) & (j < lane + EDGE)
            total += jnp.where(hit, taps(gap + (i - strip) - (j - lane)), 0.0)
    put_terms(col_ext, total)


def terms(x):
    high = x.astype(BF)
    return high, (x - high.astype(F32)).astype(BF)


def dot(a, b):
    return jnp.dot(a, b, preferred_element_type=F32)


def lanes_of(shape):
    return lax.broadcasted_iota(jnp.int32, shape, 1)


def place(x, source, target, lane):
    moved = pltpu.roll(x, (target - source) % 128, 1) if source != target else x
    return jnp.where((lane >= target) & (lane < target + EDGE), moved, 0.0)


def turned(packed):
    return jnp.transpose(
        jnp.concatenate([packed, jnp.zeros((STRIP - ROWS, 128), F32)], axis=0)
    )


def stack(ref, at, flat):
    rows = flat.shape[0]
    for t in range(STRIP // 128):
        ref[at + rows * t : at + rows * (t + 1)] = flat[:, 128 * t : 128 * t + 128]


def unstack(turn, to, ref, at, rows):
    for t in range(STRIP // 128):
        turn[to : to + rows, 128 * t : 128 * t + 128] = ref[at + rows * t : at + rows * (t + 1)]


def pack_body(ctl, wd, bm, head_dn, head_up, rest_dn, rest_up, sems):
    copies = []

    def copy(source, target):
        copies.append(pltpu.make_async_copy(source, target, sems.at[len(copies)]))
        copies[-1].start()

    for down in (True, False):
        rows = pl.ds(CY - REACH if down else 0, REACH)
        for f in range(F):
            out = (head_dn if down else head_up) if f < HEAD else (rest_dn if down else rest_up)
            copy(ctl.at[f, rows], out.at[pl.ds((f if f < HEAD else f - HEAD) * REACH, REACH)])
        out = rest_dn if down else rest_up
        for k, ref in enumerate((wd, bm)):
            copy(
                ref.at[pl.ds(CY - EXT if down else 0, EXT)],
                out.at[pl.ds((F - HEAD) * REACH + EXT * k, EXT)],
            )
    for done in copies:
        done.wait()


def parcel_body(obs, kind, live, out):
    owners, slots = obs.shape[0], obs.shape[1]
    rows = jnp.concatenate(
        [
            kind[...].astype(F32),
            jnp.broadcast_to(live[...].astype(F32), (slots, owners)),
            jnp.zeros((BLK - 2 * slots, owners), F32),
        ],
        axis=0,
    )
    for q in range(owners):
        out[(slots + 1) * q : (slots + 1) * q + slots] = obs[q]
    out[pl.ds(slots, owners, stride=slots + 1)] = jnp.transpose(rows)


def row_products(pieces, table, tile, put):
    m_high, m_low = table[0], table[1]
    for pair, columns in enumerate(pieces):
        high, low = terms(jnp.concatenate(columns, axis=1))
        size = tile + 2 * HALF
        for at in range(0, high.shape[0] - size + 1, tile):
            xh, xl = high[at : at + size], low[at : at + size]
            put(pair, at, dot(m_high, xh) + (dot(m_high, xl) + dot(m_low, xh)))


def tall_pairs(ctl, first, count, up, dn):
    for f in range(0, count, 2):
        yield [
            jnp.concatenate(
                [up[k * REACH : (k + 1) * REACH], ctl[first + k], dn[k * REACH : (k + 1) * REACH]],
                axis=0,
            )
            for k in (f, f + 1)
        ]


def row_head_body(ctl, up, dn, table, y):
    def put(pair, at, out):
        for k in range(2):
            to = (2 * pair + k) * ROWS + at
            y[to : to + 176] = out[:, 128 * k : 128 * k + 128]

    row_products(tall_pairs(ctl, 0, HEAD, up, dn), table, 176, put)


def row_rest_body(
    ctl, up, dn, wd_hbm, bm_hbm, head, table, to_left, to_right, sa, sb, wd, bm, sems
):
    loads = [
        pltpu.make_async_copy(wd_hbm, wd, sems.at[0]),
        pltpu.make_async_copy(bm_hbm, bm, sems.at[1]),
    ]
    for load in loads:
        load.start()

    def put(pair, at, out):
        for k in range(2):
            to = (2 * pair + k) * ROWS + at
            half = out[:, 128 * k : 128 * k + 128]
            to_left[to : to + 176] = half
            to_right[to : to + 176] = half

    rest = F - HEAD
    row_products(tall_pairs(ctl, HEAD, rest, up, dn), table, 176, put)
    lane = lanes_of((ROWS, 128))
    packed = jnp.zeros((ROWS, 128), F32)
    for f in range(F):
        ref, at = (head, f * ROWS) if f < HEAD else (to_left, (f - HEAD) * ROWS)
        x = ref[at : at + ROWS]
        packed += place(x, 0, EDGE * f, lane) + place(x, CX - EDGE, 32 + EDGE * f, lane)
    for load in loads:
        load.wait()
    for k, own in enumerate((wd, bm)):
        at = rest * REACH + EXT * k
        x = jnp.concatenate([up[at : at + EXT], own[...], dn[at : at + EXT]], axis=0)
        packed += place(x, 0, 64 + EDGE * k, lane) + place(x, CX - EDGE, 80 + EDGE * k, lane)
    flat = turned(packed)
    sa[...] = flat[0:32]
    sb[...] = flat[32:64]
    stack(to_left, rest * ROWS, flat[64:80])
    stack(to_right, rest * ROWS, flat[80:96])


def observe_body(values, foot, out):
    slots, owners = foot.shape
    meta = jnp.transpose(values[pl.ds(slots, owners, stride=slots + 1)])
    slot = lax.broadcasted_iota(jnp.int32, (slots, owners), 0).astype(F32)
    kind = jnp.where(meta[:slots] == 0.0, 0, CY)
    index = jnp.where(slot < meta[slots : 2 * slots], kind + foot[...], -1)
    at = jnp.concatenate([index[k : k + 1] for k in range(slots)], axis=1)
    obs = jnp.concatenate(
        [values[pl.ds(k, owners, stride=slots + 1)] for k in range(slots)], axis=0
    )
    high, low = terms(obs)
    last = (obs - high.astype(F32) - low.astype(F32)).astype(BF)
    first_pair = jnp.concatenate([high, low], axis=1)
    second_pair = jnp.concatenate([last, jnp.ones_like(last)], axis=1)
    for block in range(2 * CY // 128):
        row = lax.broadcasted_iota(jnp.int32, (128, slots * owners), 0) + 128 * block
        hot = jnp.where(row == at, 1.0, 0.0).astype(BF)
        one = dot(hot, first_pair)
        two = dot(hot, second_pair)
        out[128 * block : 128 * block + 128, :128] = one[:, :128] + (one[:, 128:] + two[:, :128])
        out[128 * block : 128 * block + 128, 128:] = two[:, 128:]


def product(x, table):
    xh, xl = terms(x)
    return dot(xh, table[0]) + (dot(xl, table[0]) + dot(xh, table[1]))


def early_body(head, left_head, right_head, rest, table, after, out):
    sides, own = table[:, : 2 * CX], table[:, 2 * CX :]
    for f in range(F):
        rows = slice(f * ROWS, (f + 1) * ROWS)
        if f < HEAD:
            near = jnp.concatenate([left_head[rows], right_head[rows]], axis=1)
            out[rows] = product(head[rows], own) + product(near, sides)
        else:
            out[rows] = product(rest[(f - HEAD) * ROWS : (f - HEAD + 1) * ROWS], own)


def middle_body(
    spot, scale, early, west_hbm, east_hbm, l2, r2, up, dn, wd, bm, tally, prec, table, ext_table,
    to_head, to_left, to_right, ext, ext_left, ext_right,
    h, u, v, b, p1, p2, q1, q2, e, gw, gb, wdx, bmx, mask, turn, left, right, sems,
):
    started = []

    def load(source, target):
        started.append(pltpu.make_async_copy(source, target, sems.at[len(started)]))
        started[-1].start()
        return started[-1]

    rest = F - HEAD
    tail = pl.ds(rest * ROWS, left.shape[0] - rest * ROWS)
    tails = [load(west_hbm.at[tail], left.at[tail]), load(east_hbm.at[tail], right.at[tail])]
    fields = []
    for f, ref in enumerate((h, u, v, b, p1, p2)):
        waits = []
        if f >= HEAD:
            rows = pl.ds((f - HEAD) * ROWS, ROWS)
            waits.append(load(west_hbm.at[rows], left.at[rows]))
            waits.append(load(east_hbm.at[rows], right.at[rows]))
        fields.append(waits)
        if f == 1:
            inner = (pl.ds(16, CY), pl.ds(0, CX))
            grids = [load(wd, wdx.at[inner]), load(bm, bmx.at[inner])]
    gx, gy, nx, ny = spot[0], spot[1], spot[2], spot[3]
    lane = lanes_of((ROWS, 128))
    turn[0:32] = l2[...]
    turn[32:64] = r2[...]
    for wait in tails:
        wait.wait()
    unstack(turn, 64, left, (F - HEAD) * ROWS, 16)
    unstack(turn, 80, right, (F - HEAD) * ROWS, 16)
    turn[96:128] = jnp.zeros((32, STRIP), F32)
    strips = jnp.transpose(turn[...])[:ROWS]
    edge = jnp.zeros((8, WIDE), F32)
    for ref in (q1, q2, e, gw, gb, mask):
        ref[0:8] = edge
        ref[TALL - 8 : TALL] = edge
    row = lax.broadcasted_iota(jnp.int32, (ROWS, WIDE), 0) - EXT
    wide_lane = lanes_of((ROWS, WIDE))
    column = jnp.where(wide_lane < WIDE * 3 // 4, wide_lane, wide_lane - WIDE)
    row += gy * CY
    column += gx * CX
    inside = (row >= 0) & (row < ny * CY) & (column >= 0) & (column < nx * CX)
    inside_f = jnp.where(inside, 1.0, 0.0)
    mask[8 : 8 + ROWS] = inside_f
    sides = table[:, : 2 * CX]
    far = product(strips, ext_table)
    for f, ref in enumerate((h, u, v, b, p1, p2)):
        if f == 2:
            for k, (wait, grid) in enumerate(zip(grids, (wdx, bmx))):
                wait.wait()
                at = (F - HEAD) * REACH + EXT * k
                grid[0:8] = edge
                grid[TALL - 8 : TALL] = edge
                grid[8:16, :128] = up[at : at + EXT]
                grid[16 + CY : 16 + CY + EXT, :128] = dn[at : at + EXT]
                grid[8 : 8 + ROWS, 128:] = place(strips, 80 + EDGE * k, 0, lane) + place(
                    strips, 64 + EDGE * k, 128 - EDGE, lane
                )
        for wait in fields[f]:
            wait.wait()
        ref[0:8] = edge
        ref[TALL - 8 : TALL] = edge
        out = early[f * ROWS : (f + 1) * ROWS]
        if f >= HEAD:
            rows = slice((f - HEAD) * ROWS, (f - HEAD + 1) * ROWS)
            out += product(jnp.concatenate([left[rows], right[rows]], axis=1), sides)
        edges = place(far, 8 * f, 128 - EDGE, lane) + place(far, 64 + 8 * f, 0, lane)
        out = jnp.concatenate([out[:, :128], out[:, 128:] + edges], axis=1) * scale[f]
        ref[8 : 8 + ROWS] = out * inside_f if f >= 4 else out
        if f == 2:
            gw[8 : 8 + ROWS] = wdx[8 : 8 + ROWS] * out
            gb[8 : 8 + ROWS] = bmx[8 : 8 + ROWS] * out

    def east_west(x):
        return pltpu.roll(x, WIDE - 1, 1), pltpu.roll(x, 1, 1)

    def slope_x(x):
        east, west = east_west(x)
        return east - west

    def at(ref, i, by=0):
        view = ref.at[pl.ds(pl.multiple_of(i * CHUNK, 8), CHUNK + 16)]
        return view[8 + by : 8 + by + CHUNK]

    def put(ref, i, value):
        ref[pl.ds(pl.multiple_of(i * CHUNK + 8, 8), CHUNK)] = value

    def slope_y(ref, i):
        return at(ref, i, 1) - at(ref, i, -1)

    def around(ref, i, centre):
        east, west = east_west(centre)
        return (at(ref, i, 1) + at(ref, i, -1)) + (east + west)

    def sweep(body):
        def step(i, carry):
            body(i)
            return carry

        lax.fori_loop(0, ROWS // CHUNK, step, 0)

    def levels(s1, s2, s1_new, s2_new):
        def body(i):
            uc = at(u, i)
            c1, c2 = at(s1, i), at(s2, i)
            hn = at(h, i) - HALF_DT * (slope_x(at(wdx, i) * uc) + slope_y(gw, i))
            bn = (
                at(b, i)
                - HALF_DT * (slope_x(at(bmx, i) * uc) + slope_y(gb, i))
                + (DT * WS[0]) * c1
                + (DT * WS[1]) * c2
            )
            put(h, i, hn)
            put(b, i, bn)
            m = at(mask, i)
            put(e, i, m * (hn + bn))
            for k, (old, c, ref) in enumerate(((s1, c1, s1_new), (s2, c2, s2_new))):
                keep = 1.0 - DT * WS[k] - 4.0 * DT * NU[k]
                put(ref, i, m * (keep * c + (DT * NU[k]) * around(old, i, c)))

        sweep(body)

    def speeds():
        def body(i):
            put(u, i, DECAY * at(u, i) - HALF_DT * slope_x(at(e, i)))
            vn = DECAY * at(v, i) - HALF_DT * slope_y(e, i)
            put(v, i, vn)
            put(gw, i, at(wdx, i) * vn)
            put(gb, i, at(bmx, i) * vn)

        sweep(body)

    levels(p1, p2, q1, q2)
    speeds()
    levels(q1, q2, p1, p2)
    speeds()
    own = slice(16, 16 + CY)
    last_u = u[own]

    def spread(grid, product):
        east, west = east_west(grid[own] * last_u)
        north_south = product[17 : 17 + CY, :128] - product[15 : 15 + CY, :128]
        return HALF_DT * ((east[:, :128] - west[:, :128]) + north_south)

    settled = (DT * WS[0]) * p1[own, :128] + (DT * WS[1]) * p2[own, :128]
    bed = b[own, :128] - spread(bmx, gb) + settled
    surface = h[own, :128] - spread(wdx, gw) + bed
    sens = []
    for k, field in enumerate((surface, bed)):
        sums = tally[k * CY : (k + 1) * CY, :128]
        count = tally[k * CY : (k + 1) * CY, 128:]
        mh, ml = terms(count * field - sums)
        rh, rl = terms(prec[k])
        sens.append(dot(mh, rh) + (dot(ml, rh) + dot(mh, rl)))
    for ref, value in ((h, sens[0]), (b, sens[0] + sens[1])):
        ref[8:16] = edge
        ref[16 + CY : 16 + CY + EXT] = edge
        ref[16 : 16 + CY, 128:] = jnp.zeros((CY, 128), F32)
        ref[16 : 16 + CY, :128] = value

    def lift():
        def body(i):
            m = at(mask, i)
            surf = (HALF_DT * m) * (slope_x(at(u, i)) + slope_y(v, i))
            put(h, i, at(h, i) + surf)
            put(b, i, at(b, i) + surf)

        sweep(body)

    def back(s1, s2, s1_new, s2_new):
        def body(i):
            hc, bc = at(h, i), at(b, i)
            depth, mobile = HALF_DT * at(wdx, i), HALF_DT * at(bmx, i)
            un = depth * slope_x(hc) + mobile * slope_x(bc)
            vn = depth * slope_y(h, i) + mobile * slope_y(b, i)
            m = at(mask, i)
            if s1 is None:
                put(u, i, un)
                put(v, i, vn)
                put(s1_new, i, (DT * WS[0]) * bc)
                put(s2_new, i, (DT * WS[1]) * bc)
            else:
                put(u, i, DECAY * at(u, i) + un)
                put(v, i, DECAY * at(v, i) + vn)
                for k, (old, new) in enumerate(((s1, s1_new), (s2, s2_new))):
                    c = at(old, i)
                    keep = 1.0 - DT * WS[k] - 4.0 * DT * NU[k]
                    put(
                        new,
                        i,
                        m * (keep * c + (DT * NU[k]) * around(old, i, c) + (DT * WS[k]) * bc),
                    )

        sweep(body)

    back(None, None, p1, p2)
    lift()
    back(p1, p2, q1, q2)
    lift()
    back(q1, q2, p1, p2)

    packed = jnp.zeros((ROWS, 128), F32)
    for f, ref in enumerate((h, u, v, b, p1, p2)):
        x = ref[8 : 8 + ROWS, :128] * scale[f]
        if f < HEAD:
            to_head[f * ROWS : (f + 1) * ROWS] = x
        else:
            to_left[(f - HEAD) * ROWS : (f - HEAD + 1) * ROWS] = x
            to_right[(f - HEAD) * ROWS : (f - HEAD + 1) * ROWS] = x
        x = ref[8 : 8 + ROWS, 128:] * scale[f]
        packed += place(x, 128 - EDGE, EDGE * f, lane) + place(x, 0, 32 + EDGE * f, lane)
    ext[...] = packed
    flat = turned(packed)
    ext_left[...] = flat[0:32]
    ext_right[...] = flat[32:64]
    stack(to_left, (F - HEAD) * ROWS, flat[0:32])
    stack(to_right, (F - HEAD) * ROWS, flat[32:64])


def column_back(fields, first, own, left, right, mine, near, far, table, z, to_up, to_dn):
    lane = lanes_of((ROWS, 128))
    th, tl = table[0], table[1]
    for k in range(fields):
        at = slice(k * ROWS, (k + 1) * ROWS)
        one, two = EDGE * (first + k), 32 + EDGE * (first + k)
        west = left[at] + (place(far, one, 0, lane) + place(mine, one, CX - EDGE, lane))
        here = own[at] + (place(near, one, 0, lane) + place(near, two, CX - EDGE, lane))
        east = right[at] + (place(mine, two, 0, lane) + place(far, two, CX - EDGE, lane))
        xh, xl = terms(jnp.concatenate([west, here, east], axis=1))
        out = dot(xh, th) + (dot(xl, th) + dot(xh, tl))
        z[k] = out
        to_up[k] = out[:REACH]
        to_dn[k] = out[ROWS - REACH :]


def column_rest_body(
    own, ext, left, right, l2, r2, table, z, to_up, to_dn, near_out, far_out, turn
):
    turn[64:128] = jnp.zeros((64, STRIP), F32)
    unstack(turn, 0, left, (F - HEAD) * ROWS, 32)
    unstack(turn, 32, right, (F - HEAD) * ROWS, 32)
    near = jnp.transpose(turn[...])[:ROWS]
    turn[0:32] = l2[...]
    turn[32:64] = r2[...]
    far = jnp.transpose(turn[...])[:ROWS]
    near_out[...] = near
    far_out[...] = far
    column_back(F - HEAD, HEAD, own, left, right, ext[...], near, far, table, z, to_up, to_dn)


def column_head_body(own, ext, left, right, near, far, table, z, to_up, to_dn):
    column_back(HEAD, 0, own, left, right, ext[...], near[...], far[...], table, z, to_up, to_dn)


def row_back_body(z_head, up_head, dn_head, z_rest, up_rest, dn_rest, ctl, table, out):
    def pairs():
        for f in range(0, F, 2):
            columns = []
            for k in (f, f + 1):
                z, up, dn, at = (
                    (z_head, up_head, dn_head, k)
                    if k < HEAD
                    else (z_rest, up_rest, dn_rest, k - HEAD)
                )
                columns.append(
                    jnp.concatenate(
                        [
                            up[at, : HALF - EXT],
                            up[at, HALF - EXT :] + z[at, : 2 * EXT],
                            z[at, 2 * EXT : ROWS - 2 * EXT],
                            z[at, ROWS - 2 * EXT :] + dn[at, : 2 * EXT],
                            dn[at, 2 * EXT :],
                        ],
                        axis=0,
                    )
                )
            yield columns

    def put(pair, at, res):
        for k in range(2):
            f = 2 * pair + k
            out[f, at : at + 256] = ctl[f, at : at + 256] + res[:, 128 * k : 128 * k + 128]

    row_products(pairs(), table, 256, put)


def call(body, outs, n_in, scratch=(), smem=0, mib=8, hbm=()):
    specs = [pl.BlockSpec(memory_space=pltpu.SMEM)] * smem
    specs += [
        pl.BlockSpec(memory_space=pltpu.HBM if i in hbm else pltpu.VMEM)
        for i in range(smem, n_in)
    ]
    run = pl.pallas_call(
        body,
        out_shape=[s if hasattr(s, "dtype") else jax.ShapeDtypeStruct(s, F32) for s in outs],
        in_specs=specs,
        out_specs=[pl.BlockSpec(memory_space=pltpu.VMEM)] * len(outs),
        scratch_shapes=list(scratch),
        compiler_params=pltpu.CompilerParams(vmem_limit_bytes=mib << 20),
    )

    def apply(*args):
        return run(
            *(
                pltpu.with_memory_space_constraint(x, pltpu.HBM) if i in hbm else x
                for i, x in enumerate(args)
            )
        )

    return apply


def send(x, axis, by):
    count = lax.axis_size(axis)
    return lax.ppermute(x, axis, [(i, i + by) for i in range(count) if 0 <= i + by < count])


def on_device(
    control, field_scale, water_depth, bed_mobility, footprint, instrument, live_counts,
    observed, obs_precision,
):
    dma = pltpu.SemaphoreType.DMA
    rest_rows = (F - HEAD) * REACH + 2 * EXT
    head_dn, head_up, rest_dn, rest_up = call(
        pack_body,
        [(HEAD * REACH, CX)] * 2 + [(rest_rows, CX)] * 2,
        3,
        [dma((2 * (F + 2),))],
        mib=3,
        hbm=(0, 1, 2),
    )(control, water_depth, bed_mobility)
    up_head = send(head_dn, GY, 1)
    dn_head = send(head_up, GY, -1)
    up_rest = send(rest_dn, GY, 1)
    dn_rest = send(rest_up, GY, -1)

    def table(*shape):
        return jax.ShapeDtypeStruct((2,) + shape, BF)

    (row_fwd,) = call(row_table_body, [table(176, 432)], 0, mib=2)()
    row_bwd, col_fwd, col_ext, col_bwd = call(
        table_body,
        [table(256, 512), table(3 * CX, WIDE), table(CX, CX), table(3 * CX, CX)],
        0,
        mib=6,
    )()

    owners, slots = instrument.shape[1:]
    lots = owners * (slots + 1)
    (parcel,) = call(parcel_body, [(lots, BLK)], 3, mib=3)(
        observed[0], jnp.swapaxes(instrument[0], 0, 1), live_counts
    )
    received = lax.all_to_all(
        parcel.reshape(owners, 1, (slots + 1) * BLK),
        (GX, GY),
        split_axis=0,
        concat_axis=0,
        tiled=True,
    ).reshape(lots, BLK)
    (tally,) = call(observe_body, [(2 * CY, 2 * BLK)], 2, mib=8)(
        received, jnp.swapaxes(footprint[0], 0, 1)
    )

    rest = F - HEAD
    (head,) = call(row_head_body, [(HEAD * ROWS, CX)], 4, mib=8)(control, up_head, dn_head, row_fwd)
    left_head = send(head, GX, 1)
    right_head = send(head, GX, -1)
    big = rest * ROWS + 16 * STRIP // 128
    y, y_right, sa, sb = call(
        row_rest_body,
        [(big, CX), (big, CX), (32, STRIP), (32, STRIP)],
        7,
        [pltpu.VMEM((CY, CX), F32)] * 2 + [dma((2,))],
        hbm=(3, 4),
    )(control, up_rest, dn_rest, water_depth, bed_mobility, head, row_fwd)
    l2 = send(sb, GX, 2)
    r2 = send(sa, GX, -2)
    left = send(y_right, GX, 1)
    right = send(y, GX, -1)

    spot = jnp.stack(
        [
            lax.axis_index(GX),
            lax.axis_index(GY),
            lax.axis_size(GX),
            lax.axis_size(GY),
        ]
    ).astype(jnp.int32)
    near_rows = big
    (early,) = call(early_body, [(F * ROWS, WIDE)], 6)(
        head, left_head, right_head, y, col_fwd, tally
    )
    big = rest * ROWS + 32 * STRIP // 128
    main_head, main, main_right, ext, ext_left, ext_right = call(
        middle_body,
        [
            (HEAD * ROWS, CX), (big, CX), (big, CX), (ROWS, CX), (32, STRIP), (32, STRIP),
        ],
        15,
        [pltpu.VMEM((TALL, WIDE), F32)] * 14 + [pltpu.VMEM((128, STRIP), F32)] + [pltpu.VMEM((near_rows, CX), F32)] * 2 + [dma((12,))],
        smem=2,
        mib=MID,
        hbm=(3, 4, 9, 10),
    )(
        spot, field_scale, early, left, right, l2, r2,
        up_rest, dn_rest, water_depth, bed_mobility, tally, obs_precision, col_fwd, col_ext,
    )

    l2 = send(ext_right, GX, 2)
    r2 = send(ext_left, GX, -2)
    left = send(main_right, GX, 1)
    right = send(main, GX, -1)
    left_head = send(main_head, GX, 1)
    right_head = send(main_head, GX, -1)
    z_rest, to_up, to_dn, near, far = call(
        column_rest_body,
        [(rest, ROWS, CX), (rest, REACH, CX), (rest, REACH, CX), (ROWS, CX), (ROWS, CX)],
        7,
        [pltpu.VMEM((128, STRIP), F32)],
    )(main, ext, left, right, l2, r2, col_bwd)
    up_rest, dn_rest = send(to_dn, GY, 1), send(to_up, GY, -1)
    z_head, to_up, to_dn = call(
        column_head_body, [(HEAD, ROWS, CX), (HEAD, REACH, CX), (HEAD, REACH, CX)], 7
    )(main_head, ext, left_head, right_head, near, far, col_bwd)
    up_head, dn_head = send(to_dn, GY, 1), send(to_up, GY, -1)
    (out,) = call(row_back_body, [(F, CY, CX)], 8)(
        z_head, up_head, dn_head, z_rest, up_rest, dn_rest, control, row_bwd
    )
    return out


def solution(mesh):
    in_specs = (
        P(None, GY, GX),
        P(),
        P(GY, GX),
        P(GY, GX),
        P((GX, GY), None, None),
        P((GX, GY), None, None),
        P((GX, GY), None),
        P((GX, GY), None, None, None),
        P(),
    )
    return jax.shard_map(
        on_device, mesh=mesh, in_specs=in_specs, out_specs=P(None, GY, GX), check_vma=False
    )
```
